1024 devices in a mesh: ctx: 256 (over z, x, core), head: 4 (over y).
Axes of the slice: x: 4, y: 4, z: 32, core: 2. Of those that a mesh axis runs over, the one named last changes fastest.
Arguments:
- query: bfloat16 [32768, 4096], P('ctx', 'head')
- key: bfloat16 [32768, 512], P(('ctx', 'head'))
- value: bfloat16 [32768, 512], P(('ctx', 'head')), may hold values from -6 to 6
- dout: bfloat16 [32768, 4096], P('ctx', 'head'), may hold values from -6 to 6
- doc_ids: int32 [32768], replicated, may hold values from 0 to 31, never falling along the last dimension, each value on 1 to 2048 neighbouring positions
- pair_flags: int32 [256, 8], P('ctx'), may hold values from 0 to 1, as said below
Outputs:
- dquery: bfloat16 [32768, 4096], P('ctx', 'head')
- dkey: bfloat16 [32768, 512], P(('ctx', 'head'))
- dvalue: bfloat16 [32768, 512], P(('ctx', 'head'))
The draws below stay inside these ranges and needn't reach their ends.
Inputs may be any that keep to these rules, and one draw needn't show every extreme that they name: `pair_flags`: column 0 is always 1; entries [b, d] with b - d < 0 are 0; for b < 8 every entry with b - d >= 0 is 1. `doc_ids`: ids never fall along the tokens.
All inputs are finite; a program needn't handle non-finite values.
Results may differ from the reference program's by a relative error of at most 0.0063.
Values may be sent and summed in bfloat16 or wider, within the bound.
No kernel may reach another device: no remote copies, remote signals or barrier semaphores. Data moves between devices by JAX's collectives and lax.ppermute only.
A program may use at most 32 MiB of HBM per device.

```python
import math
import jax
import jax.numpy as jnp
import numpy as np
from jax import lax

QH = 32
KVH = 4
HD = 128
QPK = 8
BLOCK = 128
REACH = 8
TOKENS = 32768


def draw_query(key, part):
    shape = (TOKENS, QH * HD)
    values = jax.random.normal(jax.random.fold_in(key, 11), shape, jnp.float32)
    return values.astype(jnp.bfloat16)


def draw_key(key, part):
    shape = (TOKENS, KVH * HD)
    values = jax.random.normal(jax.random.fold_in(key, 13), shape, jnp.float32)
    return values.astype(jnp.bfloat16)


def draw_pair_flags(key, part):
    block_count = TOKENS // BLOCK
    limits = jax.random.randint(jax.random.fold_in(key, 21), (block_count, 1), 1, 9)
    rolls = jax.random.randint(jax.random.fold_in(key, 22), (block_count, REACH), 0, 8)
    flags = (rolls < limits).astype(jnp.int32)
    offsets = jnp.arange(REACH, dtype=jnp.int32)[None, :]
    blocks = jnp.arange(block_count, dtype=jnp.int32)[:, None]
    flags = jnp.where(offsets == 0, 1, flags)
    flags = jnp.where(blocks < REACH, 1, flags)
    flags = jnp.where(blocks - offsets < 0, 0, flags)
    return flags.astype(jnp.int32)


def shard_levels(own_key, extent, pieces, smallest, largest):
    def one(axis_at, blocks):
        heights = jax.random.uniform(jax.random.fold_in(jax.random.fold_in(own_key, 6), axis_at), (blocks,), jnp.float32, smallest / len(pieces), largest / len(pieces))
        return jnp.repeat(jnp.exp(heights), extent[axis_at] // blocks).reshape((-1,) + (1,) * (len(extent) - axis_at - 1))

    level = one(*pieces[0])
    for cut in pieces[1:]:
        level = level * one(*cut)
    return level


def length_profile(number_of, total, most, slope):
    weights = [(1 << 20) // math.isqrt(rank ** slope) + 1 for rank in range(2, number_of + 1)]
    rest, holding = total - most - (number_of - 1), [1] * (number_of - 1)
    while rest > 0:
        movable = [i for i in range(number_of - 1) if holding[i] < most]
        whole, left = sum([weights[i] for i in movable]), rest
        for i in movable:
            more = min(most - holding[i], max(1, left * weights[i] // whole), rest)
            holding[i] = holding[i] + more
            rest = rest - more
    return np.array([most] + holding)


def uneven_parts(key, number_of, total, reach, skew):
    if number_of == 2:
        one = jax.random.randint(key, (), max(1, total - reach), min(reach, total - 1) + 1)
        return jnp.stack([one, total - one])
    tallies = jnp.asarray(length_profile(number_of, total, reach, skew), jnp.int32)
    twos = (number_of - 1) // 2
    donor, sink = tallies[1:1 + 2 * twos:2], tallies[2:2 + 2 * twos:2]
    margin = jnp.minimum(donor - 1, reach - sink)
    passed = jax.random.randint(jax.random.fold_in(key, 1), (twos,), 0, 1 << 20) % (margin + 1)
    tallies = tallies.at[1:1 + 2 * twos:2].set(donor - passed).at[2:2 + 2 * twos:2].set(sink + passed)
    return tallies[jax.random.permutation(jax.random.fold_in(key, 2), number_of)]


def scatter_about(key, dims, deviation, reach, shards=(), kind=jnp.bfloat16):
    values = jax.random.normal(key, dims, jnp.float32) * deviation
    if len(shards) > 0:
        values = shard_levels(key, dims, shards, -0.22, 0.18) * values
    return jnp.clip(values, min=-reach, max=reach).astype(kind)


def setup_inputs(seed: int = 0) -> dict:
    seeds = jax.random.split(jax.random.key(seed), 7)
    query = draw_query(jax.random.fold_in(seeds[6], 71), 0)
    key = draw_key(jax.random.fold_in(seeds[6], 71), 0)
    value = scatter_about(seeds[2], (TOKENS, KVH * HD), 1.0, 6.0, ((0, 1024),))
    dout = scatter_about(seeds[3], (TOKENS, QH * HD), 1.0, 6.0, ((0, 256), (1, 4)))
    doc_ids = jnp.searchsorted(jnp.cumsum(uneven_parts(seeds[4], TOKENS // (8 * BLOCK), TOKENS, 16 * BLOCK, 2)), jnp.arange(TOKENS), side="right").astype(jnp.int32)
    pair_flags = draw_pair_flags(jax.random.fold_in(seeds[6], 71), 0)
    return {"query": query, "key": key, "value": value, "dout": dout, "doc_ids": doc_ids, "pair_flags": pair_flags}


def allowed_mask(query_start, key_start, query_docs, key_docs, active):
    query_pos = query_start + jnp.arange(query_docs.shape[0], dtype=jnp.int32)[:, None]
    key_pos = key_start + jnp.arange(key_docs.shape[0], dtype=jnp.int32)[None, :]
    return active & (key_pos <= query_pos) & (query_docs[:, None] == key_docs[None, :])

def head_scores(query_rows, key_block, allowed, q_heads):
    inv_root = 1.0 / math.sqrt(key_block.shape[1])
    scores = jnp.dot(query_rows, key_block.T, preferred_element_type=jnp.float32) * inv_root
    scores = scores.reshape(q_heads, -1, key_block.shape[0])
    return jnp.where(allowed[None], scores, -1e+30)

def forward_step(state, query_rows, key_block, value_block, allowed, q_heads):
    top_score, total, output = state
    scores = head_scores(query_rows, key_block, allowed, q_heads)
    new_top = jnp.maximum(top_score, lax.optimization_barrier(jnp.max(scores, axis=-1, keepdims=True)))
    rescale = jnp.exp(top_score - new_top)
    probs = jnp.exp(scores - new_top)
    total = total * rescale + lax.optimization_barrier(jnp.sum(probs, axis=-1, keepdims=True))
    weighted = jnp.dot(probs.astype(jnp.bfloat16).reshape(-1, key_block.shape[0]), value_block, preferred_element_type=jnp.float32)
    output = output * rescale.reshape(-1, 1) + weighted
    return (new_top, total, output)

def finish(state, dout_rows, q_heads):
    top_score, total, output = state
    log_total = top_score + jnp.log(total)
    result = output / total.reshape(-1, 1)
    row_dot = lax.optimization_barrier(jnp.sum(dout_rows.astype(jnp.float32) * result, axis=-1)).reshape(q_heads, -1, 1)
    return (log_total, row_dot)

def backward_step(query_rows, dout_rows, key_block, value_block, allowed, log_total, row_dot, q_heads):
    inv_root = 1.0 / math.sqrt(key_block.shape[1])
    width = key_block.shape[0]
    scores = head_scores(query_rows, key_block, allowed, q_heads)
    probs = jnp.exp(scores - log_total)
    grad_probs = jnp.dot(dout_rows, value_block.T, preferred_element_type=jnp.float32).reshape(q_heads, -1, width)
    grad_scores = probs * (grad_probs - row_dot)
    probs_low = probs.astype(jnp.bfloat16).reshape(-1, width)
    grad_low = grad_scores.astype(jnp.bfloat16).reshape(-1, width)
    value_grad = jnp.dot(probs_low.T, dout_rows, preferred_element_type=jnp.float32)
    key_grad = jnp.dot(grad_low.T, query_rows, preferred_element_type=jnp.float32) * inv_root
    query_grad = jnp.dot(grad_low, key_block, preferred_element_type=jnp.float32) * inv_root
    return (query_grad, key_grad, value_grad)

def reference(query, key, value, dout, doc_ids, pair_flags):
    block_count = TOKENS // BLOCK
    q_heads = QPK
    query_grads = []
    key_grads = []
    value_grads = []
    for group in range(KVH):

        def per_block(carry, block, group=group):
            key_acc, value_acc = carry
            start = (block * BLOCK).astype(jnp.int32)
            column = jnp.int32(group * q_heads * HD)
            query_rows = lax.dynamic_slice(query, (start, column), (BLOCK, q_heads * HD))
            query_rows = query_rows.reshape(BLOCK, q_heads, HD).transpose(1, 0, 2).reshape(q_heads * BLOCK, HD)
            dout_rows = lax.dynamic_slice(dout, (start, column), (BLOCK, q_heads * HD))
            dout_rows = dout_rows.reshape(BLOCK, q_heads, HD).transpose(1, 0, 2).reshape(q_heads * BLOCK, HD)
            query_docs = lax.dynamic_slice_in_dim(doc_ids, start, BLOCK)
            paired = []
            for offset in range(REACH):
                source = ((block - offset) % block_count).astype(jnp.int32)
                key_start = (source * BLOCK).astype(jnp.int32)
                key_column = jnp.int32(group * HD)
                key_block = lax.dynamic_slice(key, (key_start, key_column), (BLOCK, HD))
                value_block = lax.dynamic_slice(value, (key_start, key_column), (BLOCK, HD))
                active = (pair_flags[block, offset] > 0) & (block - offset >= 0)
                key_docs = lax.dynamic_slice_in_dim(doc_ids, key_start, BLOCK)
                allowed = allowed_mask(start, key_start, query_docs, key_docs, active)
                paired.append((source, key_block, value_block, allowed))
            state = (jnp.full((q_heads, BLOCK, 1), -1e+30, jnp.float32), jnp.zeros((q_heads, BLOCK, 1), jnp.float32), jnp.zeros((q_heads * BLOCK, HD), jnp.float32))
            for source, key_block, value_block, allowed in paired:
                state = forward_step(state, query_rows, key_block, value_block, allowed, q_heads)
            log_total, row_dot = finish(state, dout_rows, q_heads)
            query_acc = jnp.zeros((q_heads * BLOCK, HD), jnp.float32)
            for source, key_block, value_block, allowed in paired:
                query_part, key_part, value_part = backward_step(query_rows, dout_rows, key_block, value_block, allowed, log_total, row_dot, q_heads)
                query_acc = query_acc + query_part
                key_acc = key_acc.at[source].add(key_part)
                value_acc = value_acc.at[source].add(value_part)
            block_out = query_acc.reshape(q_heads, BLOCK, HD).transpose(1, 0, 2).reshape(BLOCK, q_heads * HD)
            return ((key_acc, value_acc), block_out)
        start_acc = (jnp.zeros((block_count, BLOCK, HD), jnp.float32), jnp.zeros((block_count, BLOCK, HD), jnp.float32))
        (key_acc, value_acc), rows_out = lax.scan(per_block, start_acc, jnp.arange(block_count, dtype=jnp.int32))
        query_grads.append(rows_out.reshape(TOKENS, q_heads * HD))
        key_grads.append(key_acc.reshape(TOKENS, HD))
        value_grads.append(value_acc.reshape(TOKENS, HD))
    dquery = jnp.concatenate(query_grads, axis=1).astype(jnp.bfloat16)
    dkey = jnp.concatenate(key_grads, axis=1).astype(jnp.bfloat16)
    dvalue = jnp.concatenate(value_grads, axis=1).astype(jnp.bfloat16)
    return (dquery, dkey, dvalue)
```

```python
import math

import jax
import jax.numpy as jnp
from jax import lax
from jax.experimental import pallas as pl
from jax.experimental.pallas import tpu as pltpu
from jax.sharding import Mesh, PartitionSpec as P

HD = 128
QPK = 8
ROW = 8
VMEM = pl.BlockSpec(memory_space=pltpu.VMEM)
SMEM = pl.BlockSpec(memory_space=pltpu.SMEM)
CONTRACT_LAST = (((1,), (1,)), ((), ()))


def spread_kernel(place_ref, key_ref, value_ref, prev_ref, out_ref):
    j = place_ref[1]
    groups = key_ref.shape[1] // HD
    for g in range(groups):
        cols = slice(g * HD, (g + 1) * HD)
        own_k, own_v = key_ref[:, cols], value_ref[:, cols]
        prev_k = prev_ref[:, cols]
        prev_v = prev_ref[:, (groups + g) * HD : (groups + g + 1) * HD]
        for jp in range(ROW):
            own = j <= jp
            out_ref[jp * groups + g, :, :HD] = jnp.where(own, own_k, prev_k)
            out_ref[jp * groups + g, :, HD:] = jnp.where(own, own_v, prev_v)


def attention_kernel(
    place_ref, flags_ref, docs_ref, q_ref, do_ref, kv_ref, dq_ref, dkv_ref, cap, s_buf, dp_buf
):
    z, jp = place_ref[0], place_ref[1]
    block = q_ref.shape[0]
    root = 1.0 / math.sqrt(HD)
    to_exp2 = root * math.log2(math.e)
    own_docs = docs_ref[pl.ds(pl.multiple_of(z * ROW, ROW), ROW), :]
    prev_docs = docs_ref[pl.ds(pl.multiple_of(jnp.maximum(z - 1, 0) * ROW, ROW), ROW), :]
    row_at = lax.broadcasted_iota(jnp.int32, own_docs.shape, 0)
    query_docs = jnp.sum(jnp.where(row_at == jp, own_docs, 0), axis=0, keepdims=True)
    query_docs = query_docs.astype(jnp.float32)
    key_at = lax.broadcasted_iota(jnp.int32, (block, block), 0)
    query_at = lax.broadcasted_iota(jnp.int32, (block, block), 1)
    for j in range(ROW):
        own = j <= jp
        offset = jnp.where(own, jp - j, jp - j + ROW)
        active = (flags_ref[0, offset] > 0) & (z * ROW + jp - offset >= 0)
        docs = jnp.where(own, own_docs[j : j + 1], prev_docs[j : j + 1])
        docs = jnp.where(active, docs, -1).astype(jnp.float32)
        docs = jnp.broadcast_to(docs, (block, block)).T
        allowed = (docs == query_docs) & (key_at <= query_at + offset * block)
        cap[j * block : (j + 1) * block, :] = jnp.where(allowed, 3e38, -1e30)

    keys, values = kv_ref[:, :HD], kv_ref[:, HD:]
    keys_t = keys.T
    dk = dv = None
    for pair in range(QPK // 2):
        first, second = (slice((2 * pair + i) * HD, (2 * pair + i + 1) * HD) for i in (0, 1))
        q2 = jnp.concatenate([q_ref[:, first], q_ref[:, second]], axis=0)
        do2 = jnp.concatenate([do_ref[:, first], do_ref[:, second]], axis=0)
        s_now, dp_now = s_buf.at[pair % 2], dp_buf.at[pair % 2]
        tops = []
        for j in range(ROW):
            rows = slice(j * block, (j + 1) * block)
            s = lax.dot_general(
                kv_ref[rows, :HD], q2, CONTRACT_LAST, preferred_element_type=jnp.float32
            )
            c = cap[rows, :]
            s = jnp.minimum(s, jnp.concatenate([c, c], axis=1))
            s_now[rows, :] = s
            tops.append(jnp.max(s.reshape(-1, 8, 2 * block), axis=0))
            dp_now[rows, :] = lax.dot_general(
                kv_ref[rows, HD:], do2, CONTRACT_LAST, preferred_element_type=jnp.float32
            )
        top = tops[0]
        for t in tops[1:]:
            top = jnp.maximum(top, t)
        top = jnp.max(top, axis=0, keepdims=True)
        total = jnp.zeros((8, 2 * block), jnp.float32)
        dot = jnp.zeros((8, 2 * block), jnp.float32)
        for j in range(ROW):
            rows = slice(j * block, (j + 1) * block)
            e = jnp.exp2((s_now[rows, :] - top) * to_exp2)
            s_now[rows, :] = e
            total += jnp.sum(e.reshape(-1, 8, 2 * block), axis=0)
            dot += jnp.sum((e * dp_now[rows, :]).reshape(-1, 8, 2 * block), axis=0)
        inverse = 1.0 / jnp.sum(total, axis=0, keepdims=True)
        row_dot = jnp.sum(dot, axis=0, keepdims=True) * inverse
        probs, grads = [], []
        for j in range(ROW):
            rows = slice(j * block, (j + 1) * block)
            p = s_now[rows, :] * inverse
            probs.append(p.astype(jnp.bfloat16))
            grads.append((p * (dp_now[rows, :] - row_dot)).astype(jnp.bfloat16))
        probs = jnp.concatenate(probs, axis=0)
        grads = jnp.concatenate(grads, axis=0)
        dv_part = jnp.dot(probs, do2, preferred_element_type=jnp.float32)
        dk_part = jnp.dot(grads, q2, preferred_element_type=jnp.float32)
        dv = dv_part if dv is None else dv + dv_part
        dk = dk_part if dk is None else dk + dk_part
        dq_t = jnp.dot(keys_t, grads, preferred_element_type=jnp.float32) * root
        dq_ref[:, first] = dq_t[:, :block].T.astype(jnp.bfloat16)
        dq_ref[:, second] = dq_t[:, block:].T.astype(jnp.bfloat16)
    dkv_ref[:, :HD] = (dk * root).astype(jnp.bfloat16)
    dkv_ref[:, HD:] = dv.astype(jnp.bfloat16)


def sums_kernel(place_ref, parts_ref, own_ref, prev_ref):
    jp = place_ref[1]
    groups = parts_ref.shape[0] // ROW
    for g in range(groups):
        own = jnp.zeros(own_ref.shape[1:], jnp.float32)
        prev = jnp.zeros(own_ref.shape[1:], jnp.float32)
        for j in range(ROW):
            part = parts_ref[j * groups + g].astype(jnp.float32)
            own += jnp.where(j >= jp, part, 0.0)
            prev += jnp.where(j < jp, part, 0.0)
        own_ref[g] = own
        prev_ref[g] = prev.astype(jnp.bfloat16)


def join_kernel(own_ref, next_ref, dkey_ref, dvalue_ref):
    for g in range(own_ref.shape[0]):
        cols = slice(g * HD, (g + 1) * HD)
        both = own_ref[g] + next_ref[g].astype(jnp.float32)
        dkey_ref[:, cols] = both[:, :HD].astype(jnp.bfloat16)
        dvalue_ref[:, cols] = both[:, HD:].astype(jnp.bfloat16)


def shards(query, key, value, dout, doc_ids, pair_flags):
    shape = jax.ShapeDtypeStruct
    tokens, width = key.shape
    groups = width // HD
    block = query.shape[0]
    slots = ROW * groups
    rows = lax.axis_size("z")
    place = jnp.stack([lax.axis_index("z"), lax.axis_index("j")]).astype(jnp.int32)
    prev = lax.ppermute(
        jnp.concatenate([key, value], axis=1), "z", [(i, i + 1) for i in range(rows - 1)]
    )
    sent = pl.pallas_call(
        spread_kernel,
        out_shape=shape((slots, tokens, 2 * HD), jnp.bfloat16),
        in_specs=[SMEM, VMEM, VMEM, VMEM],
        out_specs=VMEM,
        name="spread",
    )(place, key, value, prev)
    taken = lax.all_to_all(sent, ("j", "head"), 0, 0, tiled=True)
    dquery, parts = pl.pallas_call(
        attention_kernel,
        out_shape=(
            shape(query.shape, jnp.bfloat16),
            shape((ROW * block, 2 * HD), jnp.bfloat16),
        ),
        in_specs=[SMEM, SMEM, VMEM, VMEM, VMEM, VMEM],
        out_specs=(VMEM, VMEM),
        scratch_shapes=[
            pltpu.VMEM((ROW * block, block), jnp.float32),
            pltpu.VMEM((2, ROW * block, 2 * block), jnp.float32),
            pltpu.VMEM((2, ROW * block, 2 * block), jnp.float32),
        ],
        name="attention",
    )(
        place,
        pair_flags,
        doc_ids.reshape(-1, block),
        query,
        dout,
        taken.reshape(ROW * block, 2 * HD),
    )
    back = lax.all_to_all(
        parts.reshape(slots, tokens, 2 * HD), ("j", "head"), 0, 0, tiled=True
    )
    own, to_prev = pl.pallas_call(
        sums_kernel,
        out_shape=(
            shape((groups, tokens, 2 * HD), jnp.float32),
            shape((groups, tokens, 2 * HD), jnp.bfloat16),
        ),
        in_specs=[SMEM, VMEM],
        out_specs=(VMEM, VMEM),
        name="sums",
    )(place, back)
    from_next = lax.ppermute(to_prev, "z", [(i, i - 1) for i in range(1, rows)])
    dkey, dvalue = pl.pallas_call(
        join_kernel,
        out_shape=(shape(key.shape, jnp.bfloat16), shape(value.shape, jnp.bfloat16)),
        in_specs=[VMEM, VMEM],
        out_specs=(VMEM, VMEM),
        name="join",
    )(own, from_next)
    return (dquery, dkey, dvalue)


def solution(mesh):
    ctx, head = mesh.shape["ctx"], mesh.shape["head"]
    fine = Mesh(mesh.devices.reshape(ctx // ROW, ROW, head), ("z", "j", "head"))
    by_token = P(("z", "j", "head"), None)
    in_specs = (
        P(("z", "j"), "head"),
        by_token,
        by_token,
        P(("z", "j"), "head"),
        P(),
        P(("z", "j"), None),
    )
    out_specs = (P(("z", "j"), "head"), by_token, by_token)
    return jax.shard_map(shards, mesh=fine, in_specs=in_specs, out_specs=out_specs, check_vma=False)
```

```python
import math

import jax
import jax.numpy as jnp
from jax import lax
from jax.experimental import pallas as pl
from jax.experimental.pallas import tpu as pltpu
from jax.sharding import Mesh, PartitionSpec as P

HD = 128
QPK = 8
ROW = 8
VMEM = pl.BlockSpec(memory_space=pltpu.VMEM)
SMEM = pl.BlockSpec(memory_space=pltpu.SMEM)
CONTRACT_LAST = (((1,), (1,)), ((), ()))


def spread_kernel(place_ref, key_ref, value_ref, prev_ref, out_ref):
    j = place_ref[1]
    groups = key_ref.shape[1] // HD
    for part, mine_ref in enumerate((key_ref, value_ref)):
        for g in range(groups):
            at = part * groups + g
            mine = mine_ref[:, g * HD : (g + 1) * HD]
            prev = prev_ref[:, at * HD : (at + 1) * HD]
            for jp in range(ROW):
                out_ref[jp * groups + g, :, part * HD : (part + 1) * HD] = jnp.where(
                    j <= jp, mine, prev
                )


def mask_kernel(place_ref, flags_ref, docs_ref, cap_ref):
    z, jp = place_ref[0], place_ref[1]
    block = docs_ref.shape[1]
    own_docs = docs_ref[pl.ds(pl.multiple_of(z * ROW, ROW), ROW), :]
    prev_docs = docs_ref[pl.ds(pl.multiple_of(jnp.maximum(z - 1, 0) * ROW, ROW), ROW), :]
    row_at = lax.broadcasted_iota(jnp.int32, own_docs.shape, 0)
    query_docs = jnp.sum(jnp.where(row_at == jp, own_docs, 0), axis=0, keepdims=True)
    query_docs = query_docs.astype(jnp.float32)
    key_at = lax.broadcasted_iota(jnp.int32, (block, block), 0)
    query_at = lax.broadcasted_iota(jnp.int32, (block, block), 1)
    for j in range(ROW):
        own = j <= jp
        offset = jnp.where(own, jp - j, jp - j + ROW)
        active = (flags_ref[0, offset] > 0) & (z * ROW + jp - offset >= 0)
        docs = jnp.where(own, own_docs[j : j + 1], prev_docs[j : j + 1])
        docs = jnp.where(active, docs, -1).astype(jnp.float32)
        docs = jnp.broadcast_to(docs, (block, block)).T
        allowed = (docs == query_docs) & (key_at <= query_at + offset * block)
        cap_ref[j * block : (j + 1) * block, :] = jnp.where(allowed, 3e38, -1e30)


def attention_kernel(cap_ref, q_ref, do_ref, kv_ref, dkv_ref, grads_ref, s_buf, dp_buf):
    block = q_ref.shape[0]
    root = 1.0 / math.sqrt(HD)
    to_exp2 = root * math.log2(math.e)
    dk = dv = None
    for pair in range(QPK // 2):
        first, second = (slice((2 * pair + i) * HD, (2 * pair + i + 1) * HD) for i in (0, 1))
        q2 = jnp.concatenate([q_ref[:, first], q_ref[:, second]], axis=0)
        do2 = jnp.concatenate([do_ref[:, first], do_ref[:, second]], axis=0)
        s_now, dp_now = s_buf.at[pair % 2], dp_buf.at[pair % 2]
        tops = []
        for j in range(ROW):
            rows = slice(j * block, (j + 1) * block)
            s = lax.dot_general(
                kv_ref[rows, :HD], q2, CONTRACT_LAST, preferred_element_type=jnp.float32
            )
            c = cap_ref[rows, :]
            s = jnp.minimum(s, jnp.concatenate([c, c], axis=1))
            s_now[rows, :] = s
            tops.append(jnp.max(s.reshape(-1, 8, 2 * block), axis=0))
            dp_now[rows, :] = lax.dot_general(
                kv_ref[rows, HD:], do2, CONTRACT_LAST, preferred_element_type=jnp.float32
            )
        top = tops[0]
        for t in tops[1:]:
            top = jnp.maximum(top, t)
        top = jnp.max(top, axis=0, keepdims=True)
        total = jnp.zeros((8, 2 * block), jnp.float32)
        dot = jnp.zeros((8, 2 * block), jnp.float32)
        for j in range(ROW):
            rows = slice(j * block, (j + 1) * block)
            e = jnp.exp2((s_now[rows, :] - top) * to_exp2)
            s_now[rows, :] = e
            total += jnp.sum(e.reshape(-1, 8, 2 * block), axis=0)
            dot += jnp.sum((e * dp_now[rows, :]).reshape(-1, 8, 2 * block), axis=0)
        inverse = 1.0 / jnp.sum(total, axis=0, keepdims=True)
        row_dot = jnp.sum(dot, axis=0, keepdims=True) * inverse
        probs, grads = [], []
        both = slice(2 * pair * HD, (2 * pair + 2) * HD)
        for j in range(ROW):
            rows = slice(j * block, (j + 1) * block)
            p = s_now[rows, :] * inverse
            probs.append(p.astype(jnp.bfloat16))
            grads.append((p * (dp_now[rows, :] - row_dot)).astype(jnp.bfloat16))
        probs = jnp.concatenate(probs, axis=0)
        grads = jnp.concatenate(grads, axis=0)
        dv_part = jnp.dot(probs, do2, preferred_element_type=jnp.float32)
        dk_part = jnp.dot(grads, q2, preferred_element_type=jnp.float32)
        dv = dv_part if dv is None else dv + dv_part
        dk = dk_part if dk is None else dk + dk_part
        grads_ref[:, both] = grads
    dkv_ref[:, :HD] = (dk * root).astype(jnp.bfloat16)
    dkv_ref[:, HD:] = dv.astype(jnp.bfloat16)


def dquery_kernel(kv_ref, grads_ref, dq_ref):
    block = dq_ref.shape[0]
    keys_t = kv_ref[:, :HD].T
    dq_t = jnp.dot(keys_t, grads_ref[...], preferred_element_type=jnp.float32)
    dq_t = dq_t * (1.0 / math.sqrt(HD))
    for h in range(QPK):
        cols = slice(h * HD, (h + 1) * HD)
        dq_ref[:, cols] = dq_t[:, h * block : (h + 1) * block].T.astype(jnp.bfloat16)


def sums_kernel(place_ref, parts_ref, own_ref, prev_ref):
    jp = place_ref[1]
    groups = parts_ref.shape[0] // ROW
    for g in range(groups):
        own = jnp.zeros(own_ref.shape[1:], jnp.float32)
        prev = jnp.zeros(own_ref.shape[1:], jnp.float32)
        for j in range(ROW):
            part = parts_ref[j * groups + g].astype(jnp.float32)
            own += jnp.where(j >= jp, part, 0.0)
            prev += jnp.where(j < jp, part, 0.0)
        own_ref[g] = own
        prev_ref[g] = prev.astype(jnp.bfloat16)


def join_kernel(own_ref, next_ref, dkey_ref, dvalue_ref):
    for g in range(own_ref.shape[0]):
        cols = slice(g * HD, (g + 1) * HD)
        both = own_ref[g] + next_ref[g].astype(jnp.float32)
        dkey_ref[:, cols] = both[:, :HD].astype(jnp.bfloat16)
        dvalue_ref[:, cols] = both[:, HD:].astype(jnp.bfloat16)


def held(array):
    return pltpu.with_memory_space_constraint(array, pltpu.VMEM)


def shards(query, key, value, dout, doc_ids, pair_flags):
    bf16, f32 = jnp.bfloat16, jnp.float32
    tokens, width = key.shape
    groups = width // HD
    block = query.shape[0]
    slots = ROW * groups
    rows = lax.axis_size("z")
    place = jnp.stack([lax.axis_index("z"), lax.axis_index("j")]).astype(jnp.int32)
    mine = jnp.concatenate([key, value], axis=1)
    prev = lax.ppermute(mine, "z", [(i, i + 1) for i in range(rows - 1)])
    sent = pl.pallas_call(
        spread_kernel,
        out_shape=pltpu.VMEM((slots, tokens, 2 * HD), bf16),
        in_specs=[SMEM, VMEM, VMEM, VMEM],
        out_specs=VMEM,
        compiler_params=pltpu.CompilerParams(vmem_limit_bytes=4 << 20),
        name="spread",
    )(place, held(key), held(value), held(prev))
    taken = lax.all_to_all(sent, ("j", "head"), 0, 0, tiled=True)
    taken = taken.reshape(ROW * block, 2 * HD)
    cap = pl.pallas_call(
        mask_kernel,
        out_shape=pltpu.VMEM((ROW * block, block), f32),
        in_specs=[SMEM, SMEM, VMEM],
        out_specs=VMEM,
        compiler_params=pltpu.CompilerParams(vmem_limit_bytes=4 << 20),
        name="mask",
    )(place, pair_flags, doc_ids.reshape(-1, block))
    parts, grads = pl.pallas_call(
        attention_kernel,
        out_shape=(
            pltpu.VMEM((ROW * block, 2 * HD), bf16),
            pltpu.VMEM((ROW * block, QPK * block), bf16),
        ),
        in_specs=[VMEM, VMEM, VMEM, VMEM],
        out_specs=(VMEM, VMEM),
        scratch_shapes=[pltpu.VMEM((2, ROW * block, 2 * block), f32)] * 2,
        compiler_params=pltpu.CompilerParams(vmem_limit_bytes=32 << 20),
        name="attention",
    )(held(cap), held(query), held(dout), held(taken))
    back = lax.all_to_all(
        parts.reshape(slots, tokens, 2 * HD), ("j", "head"), 0, 0, tiled=True
    )
    dquery = pl.pallas_call(
        dquery_kernel,
        out_shape=jax.ShapeDtypeStruct(query.shape, bf16),
        in_specs=[VMEM, VMEM],
        out_specs=VMEM,
        compiler_params=pltpu.CompilerParams(vmem_limit_bytes=8 << 20),
        name="dquery",
    )(held(taken), held(grads))
    own, to_prev = pl.pallas_call(
        sums_kernel,
        out_shape=(
            pltpu.VMEM((groups, tokens, 2 * HD), f32),
            pltpu.VMEM((groups, tokens, 2 * HD), bf16),
        ),
        in_specs=[SMEM, VMEM],
        out_specs=(VMEM, VMEM),
        compiler_params=pltpu.CompilerParams(vmem_limit_bytes=4 << 20),
        name="sums",
    )(place, held(back))
    from_next = lax.ppermute(to_prev, "z", [(i, i - 1) for i in range(1, rows)])
    dkey, dvalue = pl.pallas_call(
        join_kernel,
        out_shape=(
            jax.ShapeDtypeStruct(key.shape, bf16),
            jax.ShapeDtypeStruct(value.shape, bf16),
        ),
        in_specs=[VMEM, VMEM],
        out_specs=(VMEM, VMEM),
        compiler_params=pltpu.CompilerParams(vmem_limit_bytes=4 << 20),
        name="join",
    )(held(own), held(from_next))
    return (dquery, dkey, dvalue)


def solution(mesh):
    ctx, head = mesh.shape["ctx"], mesh.shape["head"]
    fine = Mesh(mesh.devices.reshape(ctx // ROW, ROW, head), ("z", "j", "head"))
    by_token = P(("z", "j", "head"), None)
    in_specs = (
        P(("z", "j"), "head"),
        by_token,
        by_token,
        P(("z", "j"), "head"),
        P(),
        P(("z", "j"), None),
    )
    out_specs = (P(("z", "j"), "head"), by_token, by_token)
    return jax.shard_map(shards, mesh=fine, in_specs=in_specs, out_specs=out_specs, check_vma=False)
```

```python
import math

import jax
import jax.numpy as jnp
from jax import lax
from jax.experimental import pallas as pl
from jax.experimental.pallas import tpu as pltpu
from jax.sharding import Mesh, PartitionSpec as P

HD = 128
QPK = 8
ROW = 8
VMEM = pl.BlockSpec(memory_space=pltpu.VMEM)
HBM = pl.BlockSpec(memory_space=pltpu.HBM)
SMEM = pl.BlockSpec(memory_space=pltpu.SMEM)
CONTRACT_LAST = (((1,), (1,)), ((), ()))


def pack_kernel(
    place_ref, key_ref, value_ref, docs_ref, flags_ref, mine_ref, rows_ref, flags_out_ref, sems
):
    z = place_ref[0]
    width = key_ref.shape[1]
    copies = [
        pltpu.make_async_copy(key_ref, mine_ref.at[:, :width], sems.at[0]),
        pltpu.make_async_copy(value_ref, mine_ref.at[:, width:], sems.at[1]),
        pltpu.make_async_copy(flags_ref, flags_out_ref, sems.at[2]),
    ]
    for at, row in enumerate((z, jnp.maximum(z - 1, 0))):
        source = docs_ref.at[pl.ds(pl.multiple_of(row * ROW, ROW), ROW), :]
        copies.append(pltpu.make_async_copy(source, rows_ref.at[at], sems.at[3 + at]))
    for copy in copies:
        copy.start()
    for copy in copies:
        copy.wait()


def spread_kernel(place_ref, mine_ref, prev_ref, out_ref):
    j = place_ref[1]
    groups = mine_ref.shape[1] // (2 * HD)
    for part in range(2):
        for g in range(groups):
            cols = slice((part * groups + g) * HD, (part * groups + g + 1) * HD)
            mine, prev = mine_ref[:, cols], prev_ref[:, cols]
            for jp in range(ROW):
                out_ref[jp * groups + g, :, part * HD : (part + 1) * HD] = jnp.where(
                    j <= jp, mine, prev
                )


def fill_cap(z, jp, rows_ref, flags_ref, cap):
    block = cap.shape[1]
    slot = lax.broadcasted_iota(jnp.int32, (ROW, block), 0)
    lane = lax.broadcasted_iota(jnp.int32, (ROW, block), 1)
    own_docs = rows_ref[0].astype(jnp.float32)
    query_docs = jnp.sum(jnp.where(slot == jp, own_docs, 0.0), axis=0, keepdims=True)
    docs = jnp.where(slot <= jp, own_docs, rows_ref[1].astype(jnp.float32))
    offset = jnp.where(slot <= jp, jp - slot, jp - slot + ROW)
    flags = jnp.concatenate([flags_ref[...]] * (block // ROW), axis=1)
    flag = jnp.where(lane == offset, jnp.broadcast_to(flags, (ROW, block)), 0)
    flag = jnp.max(flag, axis=1, keepdims=True)
    active = (flag > 0) & (z * ROW + jp - offset >= 0)
    docs = jnp.where(active, docs, -1.0)
    columns = jnp.concatenate([docs] * (block // ROW), axis=0).T
    key_at = lax.broadcasted_iota(jnp.int32, (block, block), 0)
    query_at = lax.broadcasted_iota(jnp.int32, (block, block), 1)
    ahead = key_at - query_at
    for j in range(ROW):
        reach = jnp.where(j == jp, 0, block)
        allowed = (columns[:, j : j + 1] == query_docs) & (ahead <= reach)
        cap[j * block : (j + 1) * block, :] = jnp.where(allowed, 3e38, -1e30)


def attention_kernel(
    place_ref, rows_ref, flags_ref, q_ref, do_ref, kv_ref, dkv_ref, grads_ref, cap_ref, s_buf, dp_buf
):
    fill_cap(place_ref[0], place_ref[1], rows_ref, flags_ref, cap_ref)
    block = q_ref.shape[0]
    root = 1.0 / math.sqrt(HD)
    to_exp2 = root * math.log2(math.e)
    dk = dv = None
    for pair in range(QPK // 2):
        first, second = (slice((2 * pair + i) * HD, (2 * pair + i + 1) * HD) for i in (0, 1))
        q2 = jnp.concatenate([q_ref[:, first], q_ref[:, second]], axis=0)
        do2 = jnp.concatenate([do_ref[:, first], do_ref[:, second]], axis=0)
        s_now, dp_now = s_buf.at[pair % 2], dp_buf.at[pair % 2]
        tops = []
        for j in range(ROW):
            rows = slice(j * block, (j + 1) * block)
            s = lax.dot_general(
                kv_ref[rows, :HD], q2, CONTRACT_LAST, preferred_element_type=jnp.float32
            )
            c = cap_ref[rows, :]
            s = jnp.minimum(s, jnp.concatenate([c, c], axis=1))
            s_now[rows, :] = s
            tops.append(jnp.max(s.reshape(-1, 8, 2 * block), axis=0))
            dp_now[rows, :] = lax.dot_general(
                kv_ref[rows, HD:], do2, CONTRACT_LAST, preferred_element_type=jnp.float32
            )
        top = tops[0]
        for t in tops[1:]:
            top = jnp.maximum(top, t)
        top = jnp.max(top, axis=0, keepdims=True)
        total = jnp.zeros((8, 2 * block), jnp.float32)
        dot = jnp.zeros((8, 2 * block), jnp.float32)
        for j in range(ROW):
            rows = slice(j * block, (j + 1) * block)
            e = jnp.exp2((s_now[rows, :] - top) * to_exp2)
            s_now[rows, :] = e
            total += jnp.sum(e.reshape(-1, 8, 2 * block), axis=0)
            dot += jnp.sum((e * dp_now[rows, :]).reshape(-1, 8, 2 * block), axis=0)
        inverse = 1.0 / jnp.sum(total, axis=0, keepdims=True)
        row_dot = jnp.sum(dot, axis=0, keepdims=True) * inverse
        probs, grads = [], []
        both = slice(2 * pair * HD, (2 * pair + 2) * HD)
        for j in range(ROW):
            rows = slice(j * block, (j + 1) * block)
            p = s_now[rows, :] * inverse
            probs.append(p.astype(jnp.bfloat16))
            grads.append((p * (dp_now[rows, :] - row_dot)).astype(jnp.bfloat16))
        probs = jnp.concatenate(probs, axis=0)
        grads = jnp.concatenate(grads, axis=0)
        dv_part = jnp.dot(probs, do2, preferred_element_type=jnp.float32)
        dk_part = jnp.dot(grads, q2, preferred_element_type=jnp.float32)
        dv = dv_part if dv is None else dv + dv_part
        dk = dk_part if dk is None else dk + dk_part
        grads_ref[:, both] = grads
    dkv_ref[:, :HD] = (dk * root).astype(jnp.bfloat16)
    dkv_ref[:, HD:] = dv.astype(jnp.bfloat16)


def dquery_kernel(kv_ref, grads_ref, dq_ref):
    block = dq_ref.shape[0]
    keys_t = kv_ref[:, :HD].T
    dq_t = jnp.dot(keys_t, grads_ref[...], preferred_element_type=jnp.float32)
    dq_t = dq_t * (1.0 / math.sqrt(HD))
    for h in range(QPK):
        cols = slice(h * HD, (h + 1) * HD)
        dq_ref[:, cols] = dq_t[:, h * block : (h + 1) * block].T.astype(jnp.bfloat16)


def part_sum(parts_ref, g, keep):
    groups = parts_ref.shape[0] // ROW
    total = None
    for j in range(ROW):
        part = parts_ref[j * groups + g].astype(jnp.float32)
        part = jnp.where(keep(j), part, 0.0)
        total = part if total is None else total + part
    return total


def prev_sum_kernel(place_ref, parts_ref, prev_ref):
    groups = prev_ref.shape[0]
    count = jnp.where(place_ref[0] > 0, place_ref[1], 0)

    def add(j, sums):
        return tuple(
            total + parts_ref[j * groups + g].astype(jnp.float32) for g, total in enumerate(sums)
        )

    zero = jnp.zeros(prev_ref.shape[1:], jnp.float32)
    for g, total in enumerate(lax.fori_loop(0, count, add, (zero,) * groups)):
        prev_ref[g] = total.astype(jnp.bfloat16)


def own_sum_kernel(place_ref, parts_ref, own_ref):
    jp = place_ref[1]
    for g in range(own_ref.shape[0]):
        own_ref[g] = part_sum(parts_ref, g, lambda j: j >= jp)


def join_kernel(own_ref, next_ref, dkey_ref, dvalue_ref):
    for g in range(own_ref.shape[0]):
        cols = slice(g * HD, (g + 1) * HD)
        both = own_ref[g] + next_ref[g].astype(jnp.float32)
        dkey_ref[:, cols] = both[:, :HD].astype(jnp.bfloat16)
        dvalue_ref[:, cols] = both[:, HD:].astype(jnp.bfloat16)


def held(array):
    return pltpu.with_memory_space_constraint(array, pltpu.VMEM)


def off_chip(array):
    return pltpu.with_memory_space_constraint(array, pltpu.HBM)


def shards(query, key, value, dout, doc_ids, pair_flags):
    bf16, f32 = jnp.bfloat16, jnp.float32
    tokens, width = key.shape
    groups = width // HD
    block = query.shape[0]
    slots = ROW * groups
    rows = lax.axis_size("z")
    place = jnp.stack([lax.axis_index("z"), lax.axis_index("j")]).astype(jnp.int32)
    mine, doc_rows, flags = pl.pallas_call(
        pack_kernel,
        out_shape=(
            pltpu.VMEM((tokens, 2 * width), bf16),
            pltpu.VMEM((2, ROW, block), jnp.int32),
            pltpu.VMEM(pair_flags.shape, jnp.int32),
        ),
        in_specs=[SMEM, HBM, HBM, HBM, HBM],
        out_specs=(VMEM, VMEM, VMEM),
        scratch_shapes=[pltpu.SemaphoreType.DMA((5,))],
        compiler_params=pltpu.CompilerParams(vmem_limit_bytes=4 << 20),
        name="pack",
    )(
        place,
        off_chip(key),
        off_chip(value),
        off_chip(doc_ids.reshape(-1, block)),
        off_chip(pair_flags),
    )
    passed = [(z * ROW + j, (z + 1) * ROW + j) for z in range(rows - 1) for j in range(1, ROW)]
    prev = lax.ppermute(mine, ("z", "j"), passed)
    sent = pl.pallas_call(
        spread_kernel,
        out_shape=pltpu.VMEM((slots, tokens, 2 * HD), bf16),
        in_specs=[SMEM, VMEM, VMEM],
        out_specs=VMEM,
        compiler_params=pltpu.CompilerParams(vmem_limit_bytes=4 << 20),
        name="spread",
    )(place, held(mine), held(prev))
    taken = lax.all_to_all(sent, ("j", "head"), 0, 0, tiled=True)
    taken = taken.reshape(ROW * block, 2 * HD)
    parts, grads = pl.pallas_call(
        attention_kernel,
        out_shape=(
            pltpu.VMEM((ROW * block, 2 * HD), bf16),
            pltpu.VMEM((ROW * block, QPK * block), bf16),
        ),
        in_specs=[SMEM, VMEM, VMEM, VMEM, VMEM, VMEM],
        out_specs=(VMEM, VMEM),
        scratch_shapes=[
            pltpu.VMEM((ROW * block, block), f32),
            pltpu.VMEM((2, ROW * block, 2 * block), f32),
            pltpu.VMEM((2, ROW * block, 2 * block), f32),
        ],
        compiler_params=pltpu.CompilerParams(vmem_limit_bytes=32 << 20),
        name="attention",
    )(place, held(doc_rows), held(flags), held(query), held(dout), held(taken))
    back = lax.all_to_all(
        parts.reshape(slots, tokens, 2 * HD), ("j", "head"), 0, 0, tiled=True
    )
    dquery = pl.pallas_call(
        dquery_kernel,
        out_shape=jax.ShapeDtypeStruct(query.shape, bf16),
        in_specs=[VMEM, VMEM],
        out_specs=VMEM,
        compiler_params=pltpu.CompilerParams(vmem_limit_bytes=8 << 20),
        name="dquery",
    )(held(taken), held(grads))
    to_prev = pl.pallas_call(
        prev_sum_kernel,
        out_shape=pltpu.VMEM((groups, tokens, 2 * HD), bf16),
        in_specs=[SMEM, VMEM],
        out_specs=VMEM,
        compiler_params=pltpu.CompilerParams(vmem_limit_bytes=4 << 20),
        name="prev_sum",
    )(place, held(back))
    from_next = lax.ppermute(to_prev, ("z", "j"), [(b, a) for a, b in passed])
    own = pl.pallas_call(
        own_sum_kernel,
        out_shape=pltpu.VMEM((groups, tokens, 2 * HD), f32),
        in_specs=[SMEM, VMEM],
        out_specs=VMEM,
        compiler_params=pltpu.CompilerParams(vmem_limit_bytes=4 << 20),
        name="own_sum",
    )(place, held(back))
    dkey, dvalue = pl.pallas_call(
        join_kernel,
        out_shape=(
            jax.ShapeDtypeStruct(key.shape, bf16),
            jax.ShapeDtypeStruct(value.shape, bf16),
        ),
        in_specs=[VMEM, VMEM],
        out_specs=(VMEM, VMEM),
        compiler_params=pltpu.CompilerParams(vmem_limit_bytes=4 << 20),
        name="join",
    )(held(own), held(from_next))
    return (dquery, dkey, dvalue)


def solution(mesh):
    ctx, head = mesh.shape["ctx"], mesh.shape["head"]
    fine = Mesh(mesh.devices.reshape(ctx // ROW, ROW, head), ("z", "j", "head"))
    by_token = P(("z", "j", "head"), None)
    in_specs = (
        P(("z", "j"), "head"),
        by_token,
        by_token,
        P(("z", "j"), "head"),
        P(),
        P(("z", "j"), None),
    )
    out_specs = (P(("z", "j"), "head"), by_token, by_token)
    return jax.shard_map(shards, mesh=fine, in_specs=in_specs, out_specs=out_specs, check_vma=False)
```

```python
import math

import jax
import jax.numpy as jnp
from jax import lax
from jax.experimental import pallas as pl
from jax.experimental.pallas import tpu as pltpu
from jax.sharding import Mesh, PartitionSpec as P

HD = 128
QPK = 8
ROW = 8
VMEM = pl.BlockSpec(memory_space=pltpu.VMEM)
HBM = pl.BlockSpec(memory_space=pltpu.HBM)
CHUNK = 512
CONTRACT_LAST = (((1,), (1,)), ((), ()))


def pack_kernel(key_ref, value_ref, mine_ref, sems):
    width = key_ref.shape[1]
    copies = [
        pltpu.make_async_copy(key_ref, mine_ref.at[:, :width], sems.at[0]),
        pltpu.make_async_copy(value_ref, mine_ref.at[:, width:], sems.at[1]),
    ]
    for copy in copies:
        copy.start()
    for copy in copies:
        copy.wait()


def spread_kernel(mine_ref, prev_ref, docs_ref, flags_ref, out_ref, rows_ref, flags_out_ref, sems):
    z, j = lax.axis_index("z"), lax.axis_index("j")
    copies = [pltpu.make_async_copy(flags_ref, flags_out_ref, sems.at[2])]
    for at, row in enumerate((z, jnp.maximum(z - 1, 0))):
        source = docs_ref.at[pl.ds(pl.multiple_of(row * ROW, ROW), ROW), :]
        copies.append(pltpu.make_async_copy(source, rows_ref.at[at], sems.at[at]))
    for copy in copies:
        copy.start()
    groups = mine_ref.shape[1] // (2 * HD)
    for part in range(2):
        for g in range(groups):
            cols = slice((part * groups + g) * HD, (part * groups + g + 1) * HD)
            mine, prev = mine_ref[:, cols], prev_ref[:, cols]
            for jp in range(ROW):
                out_ref[jp * groups + g, :, part * HD : (part + 1) * HD] = jnp.where(
                    j <= jp, mine, prev
                )
    for copy in copies:
        copy.wait()


def fill_cap(z, jp, rows_ref, flags_ref, cap):
    block = cap.shape[1]
    slot = lax.broadcasted_iota(jnp.int32, (ROW, block), 0)
    lane = lax.broadcasted_iota(jnp.int32, (ROW, block), 1)
    own_docs = rows_ref[0].astype(jnp.float32)
    query_docs = jnp.sum(jnp.where(slot == jp, own_docs, 0.0), axis=0, keepdims=True)
    docs = jnp.where(slot <= jp, own_docs, rows_ref[1].astype(jnp.float32))
    offset = jnp.where(slot <= jp, jp - slot, jp - slot + ROW)
    flags = jnp.concatenate([flags_ref[...]] * (block // ROW), axis=1)
    flag = jnp.where(lane == offset, jnp.broadcast_to(flags, (ROW, block)), 0)
    flag = jnp.max(flag, axis=1, keepdims=True)
    active = (flag > 0) & (z * ROW + jp - offset >= 0)
    docs = jnp.where(active, docs, -1.0)
    columns = jnp.concatenate([docs] * (block // ROW), axis=0).T
    key_at = lax.broadcasted_iota(jnp.int32, (block, block), 0)
    query_at = lax.broadcasted_iota(jnp.int32, (block, block), 1)
    ahead = key_at - query_at
    for j in range(ROW):
        reach = jnp.where(j == jp, 0, block)
        allowed = (columns[:, j : j + 1] == query_docs) & (ahead <= reach)
        cap[j * block : (j + 1) * block, :] = jnp.where(allowed, 3e38, -1e30)


def attention_kernel(
    rows_ref, flags_ref, q_ref, do_ref, kv_ref, dkv_ref, grads_ref,
    cap_ref, s_buf, dp_buf, p_buf, dk_ref, dv_ref,
):
    fill_cap(lax.axis_index("z"), lax.axis_index("j"), rows_ref, flags_ref, cap_ref)
    block = q_ref.shape[0]
    root = 1.0 / math.sqrt(HD)
    to_exp2 = root * math.log2(math.e)
    bf16, f32 = jnp.bfloat16, jnp.float32
    pairs = QPK // 2
    chunks = [slice(at, at + CHUNK) for at in range(0, kv_ref.shape[0], CHUNK)]

    def of_pair(ref, pair):
        at = 2 * pair * HD
        return jnp.concatenate([ref[:, at : at + HD], ref[:, at + HD : at + 2 * HD]], axis=0)

    def fold(array, op):
        return op(array.reshape(-1, 8, 2 * block), axis=0)

    queries = [of_pair(q_ref, pair) for pair in range(pairs)]
    douts = [of_pair(do_ref, pair) for pair in range(pairs)]

    def products(pair, rows, top):
        s = lax.dot_general(kv_ref[rows, :HD], queries[pair], CONTRACT_LAST, preferred_element_type=f32)
        c = cap_ref[rows, :]
        s = jnp.minimum(s, jnp.concatenate([c, c], axis=1))
        s_buf[pair % 2, rows, :] = s
        dp_buf[pair % 2, rows, :] = lax.dot_general(
            kv_ref[rows, HD:], douts[pair], CONTRACT_LAST, preferred_element_type=f32
        )
        s = fold(s, jnp.max)
        return s if top is None else jnp.maximum(top, s)

    def sums(pair, rows):
        probs = p_buf[pair % 2, rows, :]
        grads = grads_ref[rows, 2 * pair * block : 2 * (pair + 1) * block]
        dv = jnp.dot(probs, douts[pair], preferred_element_type=f32)
        dk = jnp.dot(grads, queries[pair], preferred_element_type=f32)
        if pair > 0:
            dv, dk = dv + dv_ref[rows, :], dk + dk_ref[rows, :]
        if pair < pairs - 1:
            dv_ref[rows, :], dk_ref[rows, :] = dv, dk
        else:
            dkv_ref[rows, :HD] = (dk * root).astype(bf16)
            dkv_ref[rows, HD:] = dv.astype(bf16)

    top = None
    for rows in chunks:
        top = products(0, rows, top)
    for pair in range(pairs):
        top_now = jnp.max(top, axis=0, keepdims=True)
        total = jnp.zeros((8, 2 * block), f32)
        dot = jnp.zeros((8, 2 * block), f32)
        top = None
        for rows in chunks:
            if pair + 1 < pairs:
                top = products(pair + 1, rows, top)
            e = jnp.exp2((s_buf[pair % 2, rows, :] - top_now) * to_exp2)
            s_buf[pair % 2, rows, :] = e
            total += fold(e, jnp.sum)
            dot += fold(e * dp_buf[pair % 2, rows, :], jnp.sum)
        inverse = 1.0 / jnp.sum(total, axis=0, keepdims=True)
        row_dot = jnp.sum(dot, axis=0, keepdims=True) * inverse
        for rows in chunks:
            if pair > 0:
                sums(pair - 1, rows)
            p = s_buf[pair % 2, rows, :] * inverse
            p_buf[pair % 2, rows, :] = p.astype(bf16)
            grads = p * (dp_buf[pair % 2, rows, :] - row_dot)
            grads_ref[rows, 2 * pair * block : 2 * (pair + 1) * block] = grads.astype(bf16)
    for rows in chunks:
        sums(pairs - 1, rows)


def dquery_kernel(kv_ref, grads_ref, dq_ref):
    block = dq_ref.shape[0]
    keys_t = kv_ref[:, :HD].T
    dq_t = jnp.dot(keys_t, grads_ref[...], preferred_element_type=jnp.float32)
    dq_t = dq_t * (1.0 / math.sqrt(HD))
    for h in range(QPK):
        cols = slice(h * HD, (h + 1) * HD)
        dq_ref[:, cols] = dq_t[:, h * block : (h + 1) * block].T.astype(jnp.bfloat16)


def part_sum(parts_ref, g, keep):
    groups = parts_ref.shape[0] // ROW
    total = None
    for j in range(ROW):
        part = parts_ref[j * groups + g].astype(jnp.float32)
        part = jnp.where(keep(j), part, 0.0)
        total = part if total is None else total + part
    return total


def prev_sum_kernel(parts_ref, prev_ref):
    groups = prev_ref.shape[0]
    count = jnp.where(lax.axis_index("z") > 0, lax.axis_index("j"), 0)

    def add(j, sums):
        return tuple(
            total + parts_ref[j * groups + g].astype(jnp.float32) for g, total in enumerate(sums)
        )

    zero = jnp.zeros(prev_ref.shape[1:], jnp.float32)
    for g, total in enumerate(lax.fori_loop(0, count, add, (zero,) * groups)):
        prev_ref[g] = total.astype(jnp.bfloat16)


def own_sum_kernel(parts_ref, own_ref):
    jp = lax.axis_index("j")
    for g in range(own_ref.shape[0]):
        own_ref[g] = part_sum(parts_ref, g, lambda j: j >= jp)


def join_kernel(own_ref, next_ref, dkey_ref, dvalue_ref):
    for g in range(own_ref.shape[0]):
        cols = slice(g * HD, (g + 1) * HD)
        both = own_ref[g] + next_ref[g].astype(jnp.float32)
        dkey_ref[:, cols] = both[:, :HD].astype(jnp.bfloat16)
        dvalue_ref[:, cols] = both[:, HD:].astype(jnp.bfloat16)


def held(array):
    return pltpu.with_memory_space_constraint(array, pltpu.VMEM)


def off_chip(array):
    return pltpu.with_memory_space_constraint(array, pltpu.HBM)


def shards(query, key, value, dout, doc_ids, pair_flags):
    bf16, f32 = jnp.bfloat16, jnp.float32
    tokens, width = key.shape
    groups = width // HD
    block = query.shape[0]
    slots = ROW * groups
    rows = lax.axis_size("z")
    mine = pl.pallas_call(
        pack_kernel,
        out_shape=pltpu.VMEM((tokens, 2 * width), bf16),
        in_specs=[HBM, HBM],
        out_specs=VMEM,
        scratch_shapes=[pltpu.SemaphoreType.DMA((2,))],
        compiler_params=pltpu.CompilerParams(vmem_limit_bytes=4 << 20),
        name="pack",
    )(off_chip(key), off_chip(value))
    passed = [(z * ROW + j, (z + 1) * ROW + j) for z in range(rows - 1) for j in range(1, ROW)]
    prev = lax.ppermute(mine, ("z", "j"), passed)
    sent, doc_rows, flags = pl.pallas_call(
        spread_kernel,
        out_shape=(
            pltpu.VMEM((slots, tokens, 2 * HD), bf16),
            pltpu.VMEM((2, ROW, block), jnp.int32),
            pltpu.VMEM(pair_flags.shape, jnp.int32),
        ),
        in_specs=[VMEM, VMEM, HBM, HBM],
        out_specs=(VMEM, VMEM, VMEM),
        scratch_shapes=[pltpu.SemaphoreType.DMA((3,))],
        compiler_params=pltpu.CompilerParams(vmem_limit_bytes=4 << 20),
        name="spread",
    )(held(mine), held(prev), off_chip(doc_ids.reshape(-1, block)), off_chip(pair_flags))
    taken = lax.all_to_all(sent, ("j", "head"), 0, 0, tiled=True)
    taken = taken.reshape(ROW * block, 2 * HD)
    parts, grads = pl.pallas_call(
        attention_kernel,
        out_shape=(
            pltpu.VMEM((ROW * block, 2 * HD), bf16),
            pltpu.VMEM((ROW * block, QPK * block), bf16),
        ),
        in_specs=[VMEM, VMEM, VMEM, VMEM, VMEM],
        out_specs=(VMEM, VMEM),
        scratch_shapes=[
            pltpu.VMEM((ROW * block, block), f32),
            pltpu.VMEM((2, ROW * block, 2 * block), f32),
            pltpu.VMEM((2, ROW * block, 2 * block), f32),
            pltpu.VMEM((2, ROW * block, 2 * block), bf16),
            pltpu.VMEM((ROW * block, HD), f32),
            pltpu.VMEM((ROW * block, HD), f32),
        ],
        compiler_params=pltpu.CompilerParams(vmem_limit_bytes=32 << 20),
        name="attention",
    )(held(doc_rows), held(flags), held(query), held(dout), held(taken))
    back = lax.all_to_all(
        parts.reshape(slots, tokens, 2 * HD), ("j", "head"), 0, 0, tiled=True
    )
    dquery = pl.pallas_call(
        dquery_kernel,
        out_shape=jax.ShapeDtypeStruct(query.shape, bf16),
        in_specs=[VMEM, VMEM],
        out_specs=VMEM,
        compiler_params=pltpu.CompilerParams(vmem_limit_bytes=8 << 20),
        name="dquery",
    )(held(taken), held(grads))
    to_prev = pl.pallas_call(
        prev_sum_kernel,
        out_shape=pltpu.VMEM((groups, tokens, 2 * HD), bf16),
        in_specs=[VMEM],
        out_specs=VMEM,
        compiler_params=pltpu.CompilerParams(vmem_limit_bytes=4 << 20),
        name="prev_sum",
    )(held(back))
    from_next = lax.ppermute(to_prev, ("z", "j"), [(b, a) for a, b in passed])
    own = pl.pallas_call(
        own_sum_kernel,
        out_shape=pltpu.VMEM((groups, tokens, 2 * HD), f32),
        in_specs=[VMEM],
        out_specs=VMEM,
        compiler_params=pltpu.CompilerParams(vmem_limit_bytes=4 << 20),
        name="own_sum",
    )(held(back))
    dkey, dvalue = pl.pallas_call(
        join_kernel,
        out_shape=(
            jax.ShapeDtypeStruct(key.shape, bf16),
            jax.ShapeDtypeStruct(value.shape, bf16),
        ),
        in_specs=[VMEM, VMEM],
        out_specs=(VMEM, VMEM),
        compiler_params=pltpu.CompilerParams(vmem_limit_bytes=4 << 20),
        name="join",
    )(held(own), held(from_next))
    return (dquery, dkey, dvalue)


def solution(mesh):
    ctx, head = mesh.shape["ctx"], mesh.shape["head"]
    fine = Mesh(mesh.devices.reshape(ctx // ROW, ROW, head), ("z", "j", "head"))
    by_token = P(("z", "j", "head"), None)
    in_specs = (
        P(("z", "j"), "head"),
        by_token,
        by_token,
        P(("z", "j"), "head"),
        P(),
        P(("z", "j"), None),
    )
    out_specs = (P(("z", "j"), "head"), by_token, by_token)
    return jax.shard_map(shards, mesh=fine, in_specs=in_specs, out_specs=out_specs, check_vma=False)
```

```python
import math

import jax
import jax.numpy as jnp
from jax import lax
from jax.experimental import pallas as pl
from jax.experimental.pallas import tpu as pltpu
from jax.sharding import Mesh, PartitionSpec as P

HD = 128
QPK = 8
ROW = 8
VMEM = pl.BlockSpec(memory_space=pltpu.VMEM)
HBM = pl.BlockSpec(memory_space=pltpu.HBM)
CHUNK = 512
CONTRACT_LAST = (((1,), (1,)), ((), ()))


def pack_kernel(
    key_ref, value_ref, docs_ref, flags_ref, q_ref, do_ref,
    mine_ref, rows_ref, flags_out_ref, q_out_ref, do_out_ref, sems,
):
    z = lax.axis_index("z")
    width = key_ref.shape[1]
    moves = [
        (key_ref, mine_ref.at[:, :width]),
        (value_ref, mine_ref.at[:, width:]),
        (flags_ref, flags_out_ref),
        (q_ref, q_out_ref),
        (do_ref, do_out_ref),
    ]
    for at, row in enumerate((z, jnp.maximum(z - 1, 0))):
        moves.append((docs_ref.at[pl.ds(pl.multiple_of(row * ROW, ROW), ROW), :], rows_ref.at[at]))
    copies = [pltpu.make_async_copy(a, b, sems.at[i]) for i, (a, b) in enumerate(moves)]
    for copy in copies:
        copy.start()
    for copy in copies:
        copy.wait()


def spread_kernel(mine_ref, prev_ref, out_ref):
    j = lax.axis_index("j")
    groups = mine_ref.shape[1] // (2 * HD)
    for part in range(2):
        for g in range(groups):
            cols = slice((part * groups + g) * HD, (part * groups + g + 1) * HD)
            mine, prev = mine_ref[:, cols], prev_ref[:, cols]
            for jp in range(ROW):
                out_ref[jp * groups + g, :, part * HD : (part + 1) * HD] = jnp.where(
                    j <= jp, mine, prev
                )


def fill_cap(z, jp, rows_ref, flags_ref, cap):
    block = cap.shape[1]
    slot = lax.broadcasted_iota(jnp.int32, (ROW, block), 0)
    lane = lax.broadcasted_iota(jnp.int32, (ROW, block), 1)
    own_docs = rows_ref[0].astype(jnp.float32)
    query_docs = jnp.sum(jnp.where(slot == jp, own_docs, 0.0), axis=0, keepdims=True)
    docs = jnp.where(slot <= jp, own_docs, rows_ref[1].astype(jnp.float32))
    offset = jnp.where(slot <= jp, jp - slot, jp - slot + ROW)
    flags = jnp.concatenate([flags_ref[...]] * (block // ROW), axis=1)
    flag = jnp.where(lane == offset, jnp.broadcast_to(flags, (ROW, block)), 0)
    flag = jnp.max(flag, axis=1, keepdims=True)
    active = (flag > 0) & (z * ROW + jp - offset >= 0)
    docs = jnp.where(active, docs, -1.0)
    columns = jnp.concatenate([docs] * (block // ROW), axis=0).T
    key_at = lax.broadcasted_iota(jnp.int32, (block, block), 0)
    query_at = lax.broadcasted_iota(jnp.int32, (block, block), 1)
    ahead = key_at - query_at
    for j in range(ROW):
        reach = jnp.where(j == jp, 0, block)
        allowed = (columns[:, j : j + 1] == query_docs) & (ahead <= reach)
        cap[j * block : (j + 1) * block, :] = jnp.where(allowed, 3e38, -1e30)


def attention_kernel(
    rows_ref, flags_ref, q_ref, do_ref, kv_ref, dkv_ref, grads_ref,
    cap_ref, s_buf, dp_buf, p_buf, dk_ref, dv_ref,
):
    fill_cap(lax.axis_index("z"), lax.axis_index("j"), rows_ref, flags_ref, cap_ref)
    block = q_ref.shape[0]
    root = 1.0 / math.sqrt(HD)
    to_exp2 = root * math.log2(math.e)
    bf16, f32 = jnp.bfloat16, jnp.float32
    pairs = QPK // 2
    chunks = [slice(at, at + CHUNK) for at in range(0, kv_ref.shape[0], CHUNK)]

    def of_pair(ref, pair):
        at = 2 * pair * HD
        return jnp.concatenate([ref[:, at : at + HD], ref[:, at + HD : at + 2 * HD]], axis=0)

    def fold(array, op):
        return op(array.reshape(-1, 8, 2 * block), axis=0)

    queries = [of_pair(q_ref, pair) for pair in range(pairs)]
    douts = [of_pair(do_ref, pair) for pair in range(pairs)]

    def products(pair, rows, top):
        s = lax.dot_general(kv_ref[rows, :HD], queries[pair], CONTRACT_LAST, preferred_element_type=f32)
        c = cap_ref[rows, :]
        s = jnp.minimum(s, jnp.concatenate([c, c], axis=1))
        s_buf[pair % 2, rows, :] = s
        dp_buf[pair % 2, rows, :] = lax.dot_general(
            kv_ref[rows, HD:], douts[pair], CONTRACT_LAST, preferred_element_type=f32
        )
        s = fold(s, jnp.max)
        return s if top is None else jnp.maximum(top, s)

    def sums(pair, rows):
        probs = p_buf[pair % 2, rows, :]
        grads = grads_ref[rows, 2 * pair * block : 2 * (pair + 1) * block]
        dv = jnp.dot(probs, douts[pair], preferred_element_type=f32)
        dk = jnp.dot(grads, queries[pair], preferred_element_type=f32)
        if pair > 0:
            dv, dk = dv + dv_ref[rows, :], dk + dk_ref[rows, :]
        if pair < pairs - 1:
            dv_ref[rows, :], dk_ref[rows, :] = dv, dk
        else:
            dkv_ref[rows, :HD] = (dk * root).astype(bf16)
            dkv_ref[rows, HD:] = dv.astype(bf16)

    top = None
    for rows in chunks:
        top = products(0, rows, top)
    for pair in range(pairs):
        top_now = jnp.max(top, axis=0, keepdims=True)
        total = jnp.zeros((8, 2 * block), f32)
        dot = jnp.zeros((8, 2 * block), f32)
        top = None
        for rows in chunks:
            if pair + 1 < pairs:
                top = products(pair + 1, rows, top)
            e = jnp.exp2((s_buf[pair % 2, rows, :] - top_now) * to_exp2)
            s_buf[pair % 2, rows, :] = e
            total += fold(e, jnp.sum)
            dot += fold(e * dp_buf[pair % 2, rows, :], jnp.sum)
        inverse = 1.0 / jnp.sum(total, axis=0, keepdims=True)
        row_dot = jnp.sum(dot, axis=0, keepdims=True) * inverse
        for rows in chunks:
            if pair > 0:
                sums(pair - 1, rows)
            p = s_buf[pair % 2, rows, :] * inverse
            p_buf[pair % 2, rows, :] = p.astype(bf16)
            grads = p * (dp_buf[pair % 2, rows, :] - row_dot)
            grads_ref[rows, 2 * pair * block : 2 * (pair + 1) * block] = grads.astype(bf16)
    for rows in chunks:
        sums(pairs - 1, rows)


def dquery_kernel(kv_ref, grads_ref, dq_ref):
    block = dq_ref.shape[0]
    keys_t = kv_ref[:, :HD].T
    dq_t = jnp.dot(keys_t, grads_ref[...], preferred_element_type=jnp.float32)
    dq_t = dq_t * (1.0 / math.sqrt(HD))
    for h in range(QPK):
        cols = slice(h * HD, (h + 1) * HD)
        dq_ref[:, cols] = dq_t[:, h * block : (h + 1) * block].T.astype(jnp.bfloat16)


def part_sum(parts_ref, g, keep):
    groups = parts_ref.shape[0] // ROW
    total = None
    for j in range(ROW):
        part = parts_ref[j * groups + g].astype(jnp.float32)
        part = jnp.where(keep(j), part, 0.0)
        total = part if total is None else total + part
    return total


def prev_sum_kernel(parts_ref, prev_ref):
    groups = prev_ref.shape[0]
    count = jnp.where(lax.axis_index("z") > 0, lax.axis_index("j"), 0)

    def add(j, sums):
        return tuple(
            total + parts_ref[j * groups + g].astype(jnp.float32) for g, total in enumerate(sums)
        )

    zero = jnp.zeros(prev_ref.shape[1:], jnp.float32)
    for g, total in enumerate(lax.fori_loop(0, count, add, (zero,) * groups)):
        prev_ref[g] = total.astype(jnp.bfloat16)


def own_sum_kernel(parts_ref, own_ref):
    jp = lax.axis_index("j")
    for g in range(own_ref.shape[0]):
        own_ref[g] = part_sum(parts_ref, g, lambda j: j >= jp)


def join_kernel(own_ref, next_ref, dkey_ref, dvalue_ref):
    for g in range(own_ref.shape[0]):
        cols = slice(g * HD, (g + 1) * HD)
        both = own_ref[g] + next_ref[g].astype(jnp.float32)
        dkey_ref[:, cols] = both[:, :HD].astype(jnp.bfloat16)
        dvalue_ref[:, cols] = both[:, HD:].astype(jnp.bfloat16)


def held(array):
    return pltpu.with_memory_space_constraint(array, pltpu.VMEM)


def off_chip(array):
    return pltpu.with_memory_space_constraint(array, pltpu.HBM)


def shards(query, key, value, dout, doc_ids, pair_flags):
    bf16, f32 = jnp.bfloat16, jnp.float32
    tokens, width = key.shape
    groups = width // HD
    block = query.shape[0]
    slots = ROW * groups
    rows = lax.axis_size("z")
    mine, doc_rows, flags, query, dout = pl.pallas_call(
        pack_kernel,
        out_shape=(
            pltpu.VMEM((tokens, 2 * width), bf16),
            pltpu.VMEM((2, ROW, block), jnp.int32),
            pltpu.VMEM(pair_flags.shape, jnp.int32),
            pltpu.VMEM(query.shape, bf16),
            pltpu.VMEM(dout.shape, bf16),
        ),
        in_specs=[HBM] * 6,
        out_specs=(VMEM,) * 5,
        scratch_shapes=[pltpu.SemaphoreType.DMA((7,))],
        compiler_params=pltpu.CompilerParams(vmem_limit_bytes=4 << 20),
        name="pack",
    )(*map(off_chip, (key, value, doc_ids.reshape(-1, block), pair_flags, query, dout)))
    passed = [(z * ROW + j, (z + 1) * ROW + j) for z in range(rows - 1) for j in range(1, ROW)]
    prev = lax.ppermute(mine, ("z", "j"), passed)
    sent = pl.pallas_call(
        spread_kernel,
        out_shape=pltpu.VMEM((slots, tokens, 2 * HD), bf16),
        in_specs=[VMEM, VMEM],
        out_specs=VMEM,
        compiler_params=pltpu.CompilerParams(vmem_limit_bytes=4 << 20),
        name="spread",
    )(held(mine), held(prev))
    taken = lax.all_to_all(sent, ("j", "head"), 0, 0, tiled=True)
    taken = taken.reshape(ROW * block, 2 * HD)
    parts, grads = pl.pallas_call(
        attention_kernel,
        out_shape=(
            pltpu.VMEM((ROW * block, 2 * HD), bf16),
            pltpu.VMEM((ROW * block, QPK * block), bf16),
        ),
        in_specs=[VMEM, VMEM, VMEM, VMEM, VMEM],
        out_specs=(VMEM, VMEM),
        scratch_shapes=[
            pltpu.VMEM((ROW * block, block), f32),
            pltpu.VMEM((2, ROW * block, 2 * block), f32),
            pltpu.VMEM((2, ROW * block, 2 * block), f32),
            pltpu.VMEM((2, ROW * block, 2 * block), bf16),
            pltpu.VMEM((ROW * block, HD), f32),
            pltpu.VMEM((ROW * block, HD), f32),
        ],
        compiler_params=pltpu.CompilerParams(vmem_limit_bytes=32 << 20),
        name="attention",
    )(held(doc_rows), held(flags), held(query), held(dout), held(taken))
    back = lax.all_to_all(
        parts.reshape(slots, tokens, 2 * HD), ("j", "head"), 0, 0, tiled=True
    )
    dquery = pl.pallas_call(
        dquery_kernel,
        out_shape=jax.ShapeDtypeStruct(query.shape, bf16),
        in_specs=[VMEM, VMEM],
        out_specs=VMEM,
        compiler_params=pltpu.CompilerParams(vmem_limit_bytes=8 << 20),
        name="dquery",
    )(held(taken), held(grads))
    to_prev = pl.pallas_call(
        prev_sum_kernel,
        out_shape=pltpu.VMEM((groups, tokens, 2 * HD), bf16),
        in_specs=[VMEM],
        out_specs=VMEM,
        compiler_params=pltpu.CompilerParams(vmem_limit_bytes=4 << 20),
        name="prev_sum",
    )(held(back))
    from_next = lax.ppermute(to_prev, ("z", "j"), [(b, a) for a, b in passed])
    own = pl.pallas_call(
        own_sum_kernel,
        out_shape=pltpu.VMEM((groups, tokens, 2 * HD), f32),
        in_specs=[VMEM],
        out_specs=VMEM,
        compiler_params=pltpu.CompilerParams(vmem_limit_bytes=4 << 20),
        name="own_sum",
    )(held(back))
    dkey, dvalue = pl.pallas_call(
        join_kernel,
        out_shape=(
            jax.ShapeDtypeStruct(key.shape, bf16),
            jax.ShapeDtypeStruct(value.shape, bf16),
        ),
        in_specs=[VMEM, VMEM],
        out_specs=(VMEM, VMEM),
        compiler_params=pltpu.CompilerParams(vmem_limit_bytes=4 << 20),
        name="join",
    )(held(own), held(from_next))
    return (dquery, dkey, dvalue)


def solution(mesh):
    ctx, head = mesh.shape["ctx"], mesh.shape["head"]
    fine = Mesh(mesh.devices.reshape(ctx // ROW, ROW, head), ("z", "j", "head"))
    by_token = P(("z", "j", "head"), None)
    in_specs = (
        P(("z", "j"), "head"),
        by_token,
        by_token,
        P(("z", "j"), "head"),
        P(),
        P(("z", "j"), None),
    )
    out_specs = (P(("z", "j"), "head"), by_token, by_token)
    return jax.shard_map(shards, mesh=fine, in_specs=in_specs, out_specs=out_specs, check_vma=False)
```

```python
import math

import jax
import jax.numpy as jnp
from jax import lax
from jax.experimental import pallas as pl
from jax.experimental.pallas import tpu as pltpu
from jax.sharding import Mesh, PartitionSpec as P

HD = 128
QPK = 8
ROW = 8
VMEM = pl.BlockSpec(memory_space=pltpu.VMEM)
HBM = pl.BlockSpec(memory_space=pltpu.HBM)
CHUNK = 512
CONTRACT_LAST = (((1,), (1,)), ((), ()))


def pack_kernel(
    key_ref, value_ref, docs_ref, flags_ref, q_ref,
    mine_ref, rows_ref, flags_out_ref, q_out_ref, sems,
):
    z = lax.axis_index("z")
    width = key_ref.shape[1]
    moves = [
        (key_ref, mine_ref.at[:, :width]),
        (value_ref, mine_ref.at[:, width:]),
        (flags_ref, flags_out_ref),
        (q_ref, q_out_ref),
    ]
    for at, row in enumerate((z, jnp.maximum(z - 1, 0))):
        moves.append((docs_ref.at[pl.ds(pl.multiple_of(row * ROW, ROW), ROW), :], rows_ref.at[at]))
    copies = [pltpu.make_async_copy(a, b, sems.at[i]) for i, (a, b) in enumerate(moves)]
    for copy in copies:
        copy.start()
    for copy in copies:
        copy.wait()


def spread_kernel(mine_ref, prev_ref, out_ref):
    j = lax.axis_index("j")
    groups = mine_ref.shape[1] // (2 * HD)
    for part in range(2):
        for g in range(groups):
            cols = slice((part * groups + g) * HD, (part * groups + g + 1) * HD)
            mine, prev = mine_ref[:, cols], prev_ref[:, cols]
            for jp in range(ROW):
                out_ref[jp * groups + g, :, part * HD : (part + 1) * HD] = jnp.where(
                    j <= jp, mine, prev
                )


def fill_cap(z, jp, rows_ref, flags_ref, cap):
    block = cap.shape[1]
    slot = lax.broadcasted_iota(jnp.int32, (ROW, block), 0)
    lane = lax.broadcasted_iota(jnp.int32, (ROW, block), 1)
    own_docs = rows_ref[0].astype(jnp.float32)
    query_docs = jnp.sum(jnp.where(slot == jp, own_docs, 0.0), axis=0, keepdims=True)
    docs = jnp.where(slot <= jp, own_docs, rows_ref[1].astype(jnp.float32))
    offset = jnp.where(slot <= jp, jp - slot, jp - slot + ROW)
    flags = jnp.concatenate([flags_ref[...]] * (block // ROW), axis=1)
    flag = jnp.where(lane == offset, jnp.broadcast_to(flags, (ROW, block)), 0)
    flag = jnp.max(flag, axis=1, keepdims=True)
    active = (flag > 0) & (z * ROW + jp - offset >= 0)
    docs = jnp.where(active, docs, -1.0)
    columns = jnp.concatenate([docs] * (block // ROW), axis=0).T
    key_at = lax.broadcasted_iota(jnp.int32, (block, block), 0)
    query_at = lax.broadcasted_iota(jnp.int32, (block, block), 1)
    ahead = key_at - query_at
    for j in range(ROW):
        reach = jnp.where(j == jp, 0, block)
        allowed = (columns[:, j : j + 1] == query_docs) & (ahead <= reach)
        cap[j * block : (j + 1) * block, :] = jnp.where(allowed, 3e38, -1e30)


def attention_kernel(
    rows_ref, flags_ref, q_ref, do_hbm, kv_ref, dkv_ref, grads_ref,
    cap_ref, s_buf, dp_buf, p_buf, dk_ref, dv_ref, do_ref, sem,
):
    fetch = pltpu.make_async_copy(do_hbm, do_ref, sem)
    fetch.start()
    fill_cap(lax.axis_index("z"), lax.axis_index("j"), rows_ref, flags_ref, cap_ref)
    fetch.wait()
    block = q_ref.shape[0]
    root = 1.0 / math.sqrt(HD)
    to_exp2 = root * math.log2(math.e)
    bf16, f32 = jnp.bfloat16, jnp.float32
    pairs = QPK // 2
    chunks = [slice(at, at + CHUNK) for at in range(0, kv_ref.shape[0], CHUNK)]

    def of_pair(ref, pair):
        at = 2 * pair * HD
        return jnp.concatenate([ref[:, at : at + HD], ref[:, at + HD : at + 2 * HD]], axis=0)

    def fold(array, op):
        return op(array.reshape(-1, 8, 2 * block), axis=0)

    queries = [of_pair(q_ref, pair) for pair in range(pairs)]
    douts = [of_pair(do_ref, pair) for pair in range(pairs)]

    def products(pair, rows, top):
        s = lax.dot_general(kv_ref[rows, :HD], queries[pair], CONTRACT_LAST, preferred_element_type=f32)
        c = cap_ref[rows, :]
        s = jnp.minimum(s, jnp.concatenate([c, c], axis=1))
        s_buf[pair % 2, rows, :] = s
        dp_buf[pair % 2, rows, :] = lax.dot_general(
            kv_ref[rows, HD:], douts[pair], CONTRACT_LAST, preferred_element_type=f32
        )
        s = fold(s, jnp.max)
        return s if top is None else jnp.maximum(top, s)

    def sums(pair, rows):
        probs = p_buf[pair % 2, rows, :]
        grads = grads_ref[rows, 2 * pair * block : 2 * (pair + 1) * block]
        dv = jnp.dot(probs, douts[pair], preferred_element_type=f32)
        dk = jnp.dot(grads, queries[pair], preferred_element_type=f32)
        if pair > 0:
            dv, dk = dv + dv_ref[rows, :], dk + dk_ref[rows, :]
        if pair < pairs - 1:
            dv_ref[rows, :], dk_ref[rows, :] = dv, dk
        else:
            dkv_ref[rows, :HD] = (dk * root).astype(bf16)
            dkv_ref[rows, HD:] = dv.astype(bf16)

    top = None
    for rows in chunks:
        top = products(0, rows, top)
    for pair in range(pairs):
        top_now = jnp.max(top, axis=0, keepdims=True)
        total = jnp.zeros((8, 2 * block), f32)
        dot = jnp.zeros((8, 2 * block), f32)
        top = None
        for rows in chunks:
            if pair + 1 < pairs:
                top = products(pair + 1, rows, top)
            e = jnp.exp2((s_buf[pair % 2, rows, :] - top_now) * to_exp2)
            s_buf[pair % 2, rows, :] = e
            total += fold(e, jnp.sum)
            dot += fold(e * dp_buf[pair % 2, rows, :], jnp.sum)
        inverse = 1.0 / jnp.sum(total, axis=0, keepdims=True)
        row_dot = jnp.sum(dot, axis=0, keepdims=True) * inverse
        for rows in chunks:
            if pair > 0:
                sums(pair - 1, rows)
            p = s_buf[pair % 2, rows, :] * inverse
            p_buf[pair % 2, rows, :] = p.astype(bf16)
            grads = p * (dp_buf[pair % 2, rows, :] - row_dot)
            grads_ref[rows, 2 * pair * block : 2 * (pair + 1) * block] = grads.astype(bf16)
    for rows in chunks:
        sums(pairs - 1, rows)


def dquery_kernel(kv_ref, grads_ref, dq_ref):
    block = dq_ref.shape[0]
    keys_t = kv_ref[:, :HD].T
    dq_t = jnp.dot(keys_t, grads_ref[...], preferred_element_type=jnp.float32)
    dq_t = dq_t * (1.0 / math.sqrt(HD))
    for h in range(QPK):
        cols = slice(h * HD, (h + 1) * HD)
        dq_ref[:, cols] = dq_t[:, h * block : (h + 1) * block].T.astype(jnp.bfloat16)


def part_sum(parts_ref, g, keep):
    groups = parts_ref.shape[0] // ROW
    total = None
    for j in range(ROW):
        part = parts_ref[j * groups + g].astype(jnp.float32)
        part = jnp.where(keep(j), part, 0.0)
        total = part if total is None else total + part
    return total


def prev_sum_kernel(parts_ref, prev_ref):
    groups = prev_ref.shape[0]
    count = jnp.where(lax.axis_index("z") > 0, lax.axis_index("j"), 0)

    def add(j, sums):
        return tuple(
            total + parts_ref[j * groups + g].astype(jnp.float32) for g, total in enumerate(sums)
        )

    zero = jnp.zeros(prev_ref.shape[1:], jnp.float32)
    for g, total in enumerate(lax.fori_loop(0, count, add, (zero,) * groups)):
        prev_ref[g] = total.astype(jnp.bfloat16)


def own_sum_kernel(parts_ref, own_ref):
    jp = lax.axis_index("j")
    for g in range(own_ref.shape[0]):
        own_ref[g] = part_sum(parts_ref, g, lambda j: j >= jp)


def join_kernel(own_ref, next_ref, dkey_ref, dvalue_ref):
    for g in range(own_ref.shape[0]):
        cols = slice(g * HD, (g + 1) * HD)
        both = own_ref[g] + next_ref[g].astype(jnp.float32)
        dkey_ref[:, cols] = both[:, :HD].astype(jnp.bfloat16)
        dvalue_ref[:, cols] = both[:, HD:].astype(jnp.bfloat16)


def held(array):
    return pltpu.with_memory_space_constraint(array, pltpu.VMEM)


def off_chip(array):
    return pltpu.with_memory_space_constraint(array, pltpu.HBM)


def shards(query, key, value, dout, doc_ids, pair_flags):
    bf16, f32 = jnp.bfloat16, jnp.float32
    tokens, width = key.shape
    groups = width // HD
    block = query.shape[0]
    slots = ROW * groups
    rows = lax.axis_size("z")
    mine, doc_rows, flags, query = pl.pallas_call(
        pack_kernel,
        out_shape=(
            pltpu.VMEM((tokens, 2 * width), bf16),
            pltpu.VMEM((2, ROW, block), jnp.int32),
            pltpu.VMEM(pair_flags.shape, jnp.int32),
            pltpu.VMEM(query.shape, bf16),
        ),
        in_specs=[HBM] * 5,
        out_specs=(VMEM,) * 4,
        scratch_shapes=[pltpu.SemaphoreType.DMA((6,))],
        compiler_params=pltpu.CompilerParams(vmem_limit_bytes=4 << 20),
        name="pack",
    )(*map(off_chip, (key, value, doc_ids.reshape(-1, block), pair_flags, query)))
    passed = [(z * ROW + j, (z + 1) * ROW + j) for z in range(rows - 1) for j in range(1, ROW)]
    prev = lax.ppermute(mine, ("z", "j"), passed)
    first_row = (lax.axis_index("z") == 0).astype(jnp.int32)
    prev, first_row = lax.optimization_barrier((prev, first_row))
    sent = pl.pallas_call(
        spread_kernel,
        out_shape=pltpu.VMEM((slots, tokens, 2 * HD), bf16),
        in_specs=[VMEM, VMEM],
        out_specs=VMEM,
        compiler_params=pltpu.CompilerParams(vmem_limit_bytes=4 << 20),
        name="spread",
    )(held(mine), held(prev))
    taken = lax.all_to_all(sent, ("j", "head"), 0, 0, tiled=True)
    taken, first_row = lax.optimization_barrier((taken, first_row))
    taken = taken.reshape(ROW * block, 2 * HD)
    parts, grads = pl.pallas_call(
        attention_kernel,
        out_shape=(
            pltpu.VMEM((ROW * block, 2 * HD), bf16),
            pltpu.VMEM((ROW * block, QPK * block), bf16),
        ),
        in_specs=[VMEM, VMEM, VMEM, HBM, VMEM],
        out_specs=(VMEM, VMEM),
        scratch_shapes=[
            pltpu.VMEM((ROW * block, block), f32),
            pltpu.VMEM((2, ROW * block, 2 * block), f32),
            pltpu.VMEM((2, ROW * block, 2 * block), f32),
            pltpu.VMEM((2, ROW * block, 2 * block), bf16),
            pltpu.VMEM((ROW * block, HD), f32),
            pltpu.VMEM((ROW * block, HD), f32),
            pltpu.VMEM(dout.shape, bf16),
            pltpu.SemaphoreType.DMA(()),
        ],
        compiler_params=pltpu.CompilerParams(vmem_limit_bytes=32 << 20),
        name="attention",
    )(held(doc_rows), held(flags), held(query), off_chip(dout), held(taken))
    exchange = lambda a: lax.all_to_all(a, ("j", "head"), 0, 0, tiled=True)
    parts = parts.reshape(slots, tokens, 2 * HD)
    back = lax.switch(first_row, (exchange, lambda a: a), parts)
    dquery = pl.pallas_call(
        dquery_kernel,
        out_shape=jax.ShapeDtypeStruct(query.shape, bf16),
        in_specs=[VMEM, VMEM],
        out_specs=VMEM,
        compiler_params=pltpu.CompilerParams(vmem_limit_bytes=8 << 20),
        name="dquery",
    )(held(taken), held(grads))
    to_prev = pl.pallas_call(
        prev_sum_kernel,
        out_shape=pltpu.VMEM((groups, tokens, 2 * HD), bf16),
        in_specs=[VMEM],
        out_specs=VMEM,
        compiler_params=pltpu.CompilerParams(vmem_limit_bytes=4 << 20),
        name="prev_sum",
    )(held(back))
    to_prev, back = lax.optimization_barrier((to_prev, back))
    from_next = lax.ppermute(to_prev, ("z", "j"), [(b, a) for a, b in passed])
    back = lax.switch(first_row, (lambda b: b, exchange), back)
    own = pl.pallas_call(
        own_sum_kernel,
        out_shape=pltpu.VMEM((groups, tokens, 2 * HD), f32),
        in_specs=[VMEM],
        out_specs=VMEM,
        compiler_params=pltpu.CompilerParams(vmem_limit_bytes=4 << 20),
        name="own_sum",
    )(held(back))
    dkey, dvalue = pl.pallas_call(
        join_kernel,
        out_shape=(
            jax.ShapeDtypeStruct(key.shape, bf16),
            jax.ShapeDtypeStruct(value.shape, bf16),
        ),
        in_specs=[VMEM, VMEM],
        out_specs=(VMEM, VMEM),
        compiler_params=pltpu.CompilerParams(vmem_limit_bytes=4 << 20),
        name="join",
    )(held(own), held(from_next))
    return (dquery, dkey, dvalue)


def solution(mesh):
    ctx, head = mesh.shape["ctx"], mesh.shape["head"]
    fine = Mesh(mesh.devices.reshape(ctx // ROW, ROW, head), ("z", "j", "head"))
    by_token = P(("z", "j", "head"), None)
    in_specs = (
        P(("z", "j"), "head"),
        by_token,
        by_token,
        P(("z", "j"), "head"),
        P(),
        P(("z", "j"), None),
    )
    out_specs = (P(("z", "j"), "head"), by_token, by_token)
    return jax.shard_map(shards, mesh=fine, in_specs=in_specs, out_specs=out_specs, check_vma=False)
```

```python
import math

import jax
import jax.numpy as jnp
from jax import lax
from jax.experimental import pallas as pl
from jax.experimental.pallas import tpu as pltpu
from jax.sharding import Mesh, PartitionSpec as P

HD = 128
QPK = 8
ROW = 8
VMEM = pl.BlockSpec(memory_space=pltpu.VMEM)
HBM = pl.BlockSpec(memory_space=pltpu.HBM)
CHUNK = 512
CONTRACT_LAST = (((1,), (1,)), ((), ()))


def pack_kernel(
    key_ref, value_ref, docs_ref, flags_ref, q_ref,
    mine_ref, rows_ref, flags_out_ref, q_out_ref, sems,
):
    z = lax.axis_index("z")
    width = key_ref.shape[1]
    moves = [
        (key_ref, mine_ref.at[:, :width]),
        (value_ref, mine_ref.at[:, width:]),
        (flags_ref, flags_out_ref),
        (q_ref, q_out_ref),
    ]
    for at, row in enumerate((z, jnp.maximum(z - 1, 0))):
        moves.append((docs_ref.at[pl.ds(pl.multiple_of(row * ROW, ROW), ROW), :], rows_ref.at[at]))
    copies = [pltpu.make_async_copy(a, b, sems.at[i]) for i, (a, b) in enumerate(moves)]
    for copy in copies:
        copy.start()
    for copy in copies:
        copy.wait()


def spread_kernel(mine_ref, prev_ref, out_ref):
    j = lax.axis_index("j")
    groups = mine_ref.shape[1] // (2 * HD)
    for part in range(2):
        for g in range(groups):
            cols = slice((part * groups + g) * HD, (part * groups + g + 1) * HD)
            mine, prev = mine_ref[:, cols], prev_ref[:, cols]
            for jp in range(ROW):
                out_ref[jp * groups + g, :, part * HD : (part + 1) * HD] = jnp.where(
                    j <= jp, mine, prev
                )


def fill_cap(z, jp, rows_ref, flags_ref, cap):
    block = cap.shape[1]
    slot = lax.broadcasted_iota(jnp.int32, (ROW, block), 0)
    lane = lax.broadcasted_iota(jnp.int32, (ROW, block), 1)
    own_docs = rows_ref[0].astype(jnp.float32)
    query_docs = jnp.sum(jnp.where(slot == jp, own_docs, 0.0), axis=0, keepdims=True)
    docs = jnp.where(slot <= jp, own_docs, rows_ref[1].astype(jnp.float32))
    offset = jnp.where(slot <= jp, jp - slot, jp - slot + ROW)
    flags = jnp.concatenate([flags_ref[...]] * (block // ROW), axis=1)
    flag = jnp.where(lane == offset, jnp.broadcast_to(flags, (ROW, block)), 0)
    flag = jnp.max(flag, axis=1, keepdims=True)
    active = (flag > 0) & (z * ROW + jp - offset >= 0)
    docs = jnp.where(active, docs, -1.0)
    columns = jnp.concatenate([docs] * (block // ROW), axis=0).T
    key_at = lax.broadcasted_iota(jnp.int32, (block, block), 0)
    query_at = lax.broadcasted_iota(jnp.int32, (block, block), 1)
    ahead = key_at - query_at
    for j in range(ROW):
        reach = jnp.where(j == jp, 0, block)
        allowed = (columns[:, j : j + 1] == query_docs) & (ahead <= reach)
        cap[j * block : (j + 1) * block, :] = jnp.where(allowed, 3e38, -1e30)


def attention_kernel(
    rows_ref, flags_ref, q_ref, do_hbm, kv_ref, dkv_ref, grads_ref,
    cap_ref, s_buf, dp_buf, p_buf, dk_ref, dv_ref, do_ref, sem,
):
    fetch = pltpu.make_async_copy(do_hbm, do_ref, sem)
    fetch.start()
    fill_cap(lax.axis_index("z"), lax.axis_index("j"), rows_ref, flags_ref, cap_ref)
    block = q_ref.shape[0]
    root = 1.0 / math.sqrt(HD)
    to_exp2 = root * math.log2(math.e)
    bf16, f32 = jnp.bfloat16, jnp.float32
    pairs = QPK // 2
    chunks = [slice(at, at + CHUNK) for at in range(0, kv_ref.shape[0], CHUNK)]

    def of_pair(ref, pair):
        at = 2 * pair * HD
        return jnp.concatenate([ref[:, at : at + HD], ref[:, at + HD : at + 2 * HD]], axis=0)

    def fold(array, op):
        return op(array.reshape(-1, 8, 2 * block), axis=0)

    queries = [of_pair(q_ref, pair) for pair in range(pairs)]
    douts = []

    def scores(pair, rows, top):
        s = lax.dot_general(kv_ref[rows, :HD], queries[pair], CONTRACT_LAST, preferred_element_type=f32)
        c = cap_ref[rows, :]
        s = jnp.minimum(s, jnp.concatenate([c, c], axis=1))
        s_buf[pair % 2, rows, :] = s
        s = fold(s, jnp.max)
        return s if top is None else jnp.maximum(top, s)

    def dout_products(pair, rows):
        dp_buf[pair % 2, rows, :] = lax.dot_general(
            kv_ref[rows, HD:], douts[pair], CONTRACT_LAST, preferred_element_type=f32
        )

    def sums(pair, rows):
        probs = p_buf[pair % 2, rows, :]
        grads = grads_ref[rows, 2 * pair * block : 2 * (pair + 1) * block]
        dv = jnp.dot(probs, douts[pair], preferred_element_type=f32)
        dk = jnp.dot(grads, queries[pair], preferred_element_type=f32)
        if pair > 0:
            dv, dk = dv + dv_ref[rows, :], dk + dk_ref[rows, :]
        if pair < pairs - 1:
            dv_ref[rows, :], dk_ref[rows, :] = dv, dk
        else:
            dkv_ref[rows, :HD] = (dk * root).astype(bf16)
            dkv_ref[rows, HD:] = dv.astype(bf16)

    top = None
    for rows in chunks:
        top = scores(0, rows, top)
    fetch.wait()
    douts.extend(of_pair(do_ref, pair) for pair in range(pairs))
    for rows in chunks:
        dout_products(0, rows)
    for pair in range(pairs):
        top_now = jnp.max(top, axis=0, keepdims=True)
        total = jnp.zeros((8, 2 * block), f32)
        dot = jnp.zeros((8, 2 * block), f32)
        top = None
        for rows in chunks:
            if pair + 1 < pairs:
                top = scores(pair + 1, rows, top)
                dout_products(pair + 1, rows)
            e = jnp.exp2((s_buf[pair % 2, rows, :] - top_now) * to_exp2)
            s_buf[pair % 2, rows, :] = e
            total += fold(e, jnp.sum)
            dot += fold(e * dp_buf[pair % 2, rows, :], jnp.sum)
        inverse = 1.0 / jnp.sum(total, axis=0, keepdims=True)
        row_dot = jnp.sum(dot, axis=0, keepdims=True) * inverse
        for rows in chunks:
            if pair > 0:
                sums(pair - 1, rows)
            p = s_buf[pair % 2, rows, :] * inverse
            p_buf[pair % 2, rows, :] = p.astype(bf16)
            grads = p * (dp_buf[pair % 2, rows, :] - row_dot)
            grads_ref[rows, 2 * pair * block : 2 * (pair + 1) * block] = grads.astype(bf16)
    for rows in chunks:
        sums(pairs - 1, rows)


def dquery_kernel(kv_ref, grads_ref, dq_ref):
    block = dq_ref.shape[0]
    keys_t = kv_ref[:, :HD].T
    dq_t = jnp.dot(keys_t, grads_ref[...], preferred_element_type=jnp.float32)
    dq_t = dq_t * (1.0 / math.sqrt(HD))
    for h in range(QPK):
        cols = slice(h * HD, (h + 1) * HD)
        dq_ref[:, cols] = dq_t[:, h * block : (h + 1) * block].T.astype(jnp.bfloat16)


def part_sum(parts_ref, g, keep):
    groups = parts_ref.shape[0] // ROW
    total = None
    for j in range(ROW):
        part = parts_ref[j * groups + g].astype(jnp.float32)
        part = jnp.where(keep(j), part, 0.0)
        total = part if total is None else total + part
    return total


def prev_sum_kernel(parts_ref, prev_ref):
    groups = prev_ref.shape[0]
    count = jnp.where(lax.axis_index("z") > 0, lax.axis_index("j"), 0)

    def add(j, sums):
        return tuple(
            total + parts_ref[j * groups + g].astype(jnp.float32) for g, total in enumerate(sums)
        )

    zero = jnp.zeros(prev_ref.shape[1:], jnp.float32)
    for g, total in enumerate(lax.fori_loop(0, count, add, (zero,) * groups)):
        prev_ref[g] = total.astype(jnp.bfloat16)


def own_sum_kernel(parts_ref, own_ref):
    jp = lax.axis_index("j")
    for g in range(own_ref.shape[0]):
        own_ref[g] = part_sum(parts_ref, g, lambda j: j >= jp)


def join_kernel(own_ref, next_ref, dkey_ref, dvalue_ref):
    for g in range(own_ref.shape[0]):
        cols = slice(g * HD, (g + 1) * HD)
        both = own_ref[g] + next_ref[g].astype(jnp.float32)
        dkey_ref[:, cols] = both[:, :HD].astype(jnp.bfloat16)
        dvalue_ref[:, cols] = both[:, HD:].astype(jnp.bfloat16)


def held(array):
    return pltpu.with_memory_space_constraint(array, pltpu.VMEM)


def off_chip(array):
    return pltpu.with_memory_space_constraint(array, pltpu.HBM)


def shards(query, key, value, dout, doc_ids, pair_flags):
    bf16, f32 = jnp.bfloat16, jnp.float32
    tokens, width = key.shape
    groups = width // HD
    block = query.shape[0]
    slots = ROW * groups
    rows = lax.axis_size("z")
    mine, doc_rows, flags, query = pl.pallas_call(
        pack_kernel,
        out_shape=(
            pltpu.VMEM((tokens, 2 * width), bf16),
            pltpu.VMEM((2, ROW, block), jnp.int32),
            pltpu.VMEM(pair_flags.shape, jnp.int32),
            pltpu.VMEM(query.shape, bf16),
        ),
        in_specs=[HBM] * 5,
        out_specs=(VMEM,) * 4,
        scratch_shapes=[pltpu.SemaphoreType.DMA((6,))],
        compiler_params=pltpu.CompilerParams(vmem_limit_bytes=4 << 20),
        name="pack",
    )(*map(off_chip, (key, value, doc_ids.reshape(-1, block), pair_flags, query)))
    passed = [(z * ROW + j, (z + 1) * ROW + j) for z in range(rows - 1) for j in range(1, ROW)]
    prev = lax.ppermute(mine, ("z", "j"), passed)
    first_row = (lax.axis_index("z") == 0).astype(jnp.int32)
    prev, first_row = lax.optimization_barrier((prev, first_row))
    sent = pl.pallas_call(
        spread_kernel,
        out_shape=pltpu.VMEM((slots, tokens, 2 * HD), bf16),
        in_specs=[VMEM, VMEM],
        out_specs=VMEM,
        compiler_params=pltpu.CompilerParams(vmem_limit_bytes=4 << 20),
        name="spread",
    )(held(mine), held(prev))
    taken = lax.all_to_all(sent, ("j", "head"), 0, 0, tiled=True)
    taken, first_row = lax.optimization_barrier((taken, first_row))
    taken = taken.reshape(ROW * block, 2 * HD)
    parts, grads = pl.pallas_call(
        attention_kernel,
        out_shape=(
            pltpu.VMEM((ROW * block, 2 * HD), bf16),
            pltpu.VMEM((ROW * block, QPK * block), bf16),
        ),
        in_specs=[VMEM, VMEM, VMEM, HBM, VMEM],
        out_specs=(VMEM, VMEM),
        scratch_shapes=[
            pltpu.VMEM((ROW * block, block), f32),
            pltpu.VMEM((2, ROW * block, 2 * block), f32),
            pltpu.VMEM((2, ROW * block, 2 * block), f32),
            pltpu.VMEM((2, ROW * block, 2 * block), bf16),
            pltpu.VMEM((ROW * block, HD), f32),
            pltpu.VMEM((ROW * block, HD), f32),
            pltpu.VMEM(dout.shape, bf16),
            pltpu.SemaphoreType.DMA(()),
        ],
        compiler_params=pltpu.CompilerParams(vmem_limit_bytes=32 << 20),
        name="attention",
    )(held(doc_rows), held(flags), held(query), off_chip(dout), held(taken))
    exchange = lambda a: lax.all_to_all(a, ("j", "head"), 0, 0, tiled=True)
    parts = parts.reshape(slots, tokens, 2 * HD)
    back = lax.switch(first_row, (exchange, lambda a: a), parts)
    dquery = pl.pallas_call(
        dquery_kernel,
        out_shape=jax.ShapeDtypeStruct(query.shape, bf16),
        in_specs=[VMEM, VMEM],
        out_specs=VMEM,
        compiler_params=pltpu.CompilerParams(vmem_limit_bytes=8 << 20),
        name="dquery",
    )(held(taken), held(grads))
    to_prev = pl.pallas_call(
        prev_sum_kernel,
        out_shape=pltpu.VMEM((groups, tokens, 2 * HD), bf16),
        in_specs=[VMEM],
        out_specs=VMEM,
        compiler_params=pltpu.CompilerParams(vmem_limit_bytes=4 << 20),
        name="prev_sum",
    )(held(back))
    to_prev, back = lax.optimization_barrier((to_prev, back))
    from_next = lax.ppermute(to_prev, ("z", "j"), [(b, a) for a, b in passed])
    back = lax.switch(first_row, (lambda b: b, exchange), back)
    own = pl.pallas_call(
        own_sum_kernel,
        out_shape=pltpu.VMEM((groups, tokens, 2 * HD), f32),
        in_specs=[VMEM],
        out_specs=VMEM,
        compiler_params=pltpu.CompilerParams(vmem_limit_bytes=4 << 20),
        name="own_sum",
    )(held(back))
    dkey, dvalue = pl.pallas_call(
        join_kernel,
        out_shape=(
            jax.ShapeDtypeStruct(key.shape, bf16),
            jax.ShapeDtypeStruct(value.shape, bf16),
        ),
        in_specs=[VMEM, VMEM],
        out_specs=(VMEM, VMEM),
        compiler_params=pltpu.CompilerParams(vmem_limit_bytes=4 << 20),
        name="join",
    )(held(own), held(from_next))
    return (dquery, dkey, dvalue)


def solution(mesh):
    ctx, head = mesh.shape["ctx"], mesh.shape["head"]
    fine = Mesh(mesh.devices.reshape(ctx // ROW, ROW, head), ("z", "j", "head"))
    by_token = P(("z", "j", "head"), None)
    in_specs = (
        P(("z", "j"), "head"),
        by_token,
        by_token,
        P(("z", "j"), "head"),
        P(),
        P(("z", "j"), None),
    )
    out_specs = (P(("z", "j"), "head"), by_token, by_token)
    return jax.shard_map(shards, mesh=fine, in_specs=in_specs, out_specs=out_specs, check_vma=False)
```

```python
import math

import jax
import jax.numpy as jnp
from jax import lax
from jax.experimental import pallas as pl
from jax.experimental.pallas import tpu as pltpu
from jax.sharding import Mesh, PartitionSpec as P

HD = 128
QPK = 8
ROW = 8
VMEM = pl.BlockSpec(memory_space=pltpu.VMEM)
HBM = pl.BlockSpec(memory_space=pltpu.HBM)
CHUNK = 512
CONTRACT_LAST = (((1,), (1,)), ((), ()))


def pack_kernel(
    key_ref, value_ref, docs_ref, flags_ref, q_ref, do_ref,
    mine_ref, rows_ref, flags_out_ref, q_out_ref, do_out_ref, sems,
):
    z = lax.axis_index("z")
    width = key_ref.shape[1]
    moves = [
        (key_ref, mine_ref.at[:, :width]),
        (value_ref, mine_ref.at[:, width:]),
        (flags_ref, flags_out_ref),
        (q_ref, q_out_ref),
        (do_ref, do_out_ref),
    ]
    for at, row in enumerate((z, jnp.maximum(z - 1, 0))):
        moves.append((docs_ref.at[pl.ds(pl.multiple_of(row * ROW, ROW), ROW), :], rows_ref.at[at]))
    copies = [pltpu.make_async_copy(a, b, sems.at[i]) for i, (a, b) in enumerate(moves)]
    for copy in copies:
        copy.start()
    for copy in copies:
        copy.wait()


def spread_kernel(mine_ref, prev_ref, out_ref):
    j = lax.axis_index("j")
    groups = mine_ref.shape[1] // (2 * HD)
    for part in range(2):
        for g in range(groups):
            cols = slice((part * groups + g) * HD, (part * groups + g + 1) * HD)
            mine, prev = mine_ref[:, cols], prev_ref[:, cols]
            for jp in range(ROW):
                out_ref[jp * groups + g, :, part * HD : (part + 1) * HD] = jnp.where(
                    j <= jp, mine, prev
                )


def fill_cap(z, jp, rows_ref, flags_ref, cap):
    block = cap.shape[1]
    slot = lax.broadcasted_iota(jnp.int32, (ROW, block), 0)
    lane = lax.broadcasted_iota(jnp.int32, (ROW, block), 1)
    own_docs = rows_ref[0].astype(jnp.float32)
    query_docs = jnp.sum(jnp.where(slot == jp, own_docs, 0.0), axis=0, keepdims=True)
    docs = jnp.where(slot <= jp, own_docs, rows_ref[1].astype(jnp.float32))
    offset = jnp.where(slot <= jp, jp - slot, jp - slot + ROW)
    flags = jnp.concatenate([flags_ref[...]] * (block // ROW), axis=1)
    flag = jnp.where(lane == offset, jnp.broadcast_to(flags, (ROW, block)), 0)
    flag = jnp.max(flag, axis=1, keepdims=True)
    active = (flag > 0) & (z * ROW + jp - offset >= 0)
    docs = jnp.where(active, docs, -1.0)
    columns = jnp.concatenate([docs] * (block // ROW), axis=0).T
    key_at = lax.broadcasted_iota(jnp.int32, (block, block), 0)
    query_at = lax.broadcasted_iota(jnp.int32, (block, block), 1)
    ahead = key_at - query_at
    for j in range(ROW):
        reach = jnp.where(j == jp, 0, block)
        allowed = (columns[:, j : j + 1] == query_docs) & (ahead <= reach)
        cap[j * block : (j + 1) * block, :] = jnp.where(allowed, 3e38, -1e30)


def attention_kernel(
    rows_ref, flags_ref, q_ref, do_ref, kv_ref, dkv_ref, grads_ref, dq_last_ref,
    cap_ref, s_buf, dp_buf, p_buf, dk_ref, dv_ref, last_ref,
):
    fill_cap(lax.axis_index("z"), lax.axis_index("j"), rows_ref, flags_ref, cap_ref)
    block = q_ref.shape[0]
    root = 1.0 / math.sqrt(HD)
    to_exp2 = root * math.log2(math.e)
    bf16, f32 = jnp.bfloat16, jnp.float32
    pairs = QPK // 2
    chunks = [slice(at, at + CHUNK) for at in range(0, kv_ref.shape[0], CHUNK)]

    def of_pair(ref, pair):
        at = 2 * pair * HD
        return jnp.concatenate([ref[:, at : at + HD], ref[:, at + HD : at + 2 * HD]], axis=0)

    def fold(array, op):
        return op(array.reshape(-1, 8, 2 * block), axis=0)

    queries = [of_pair(q_ref, pair) for pair in range(pairs)]
    douts = [of_pair(do_ref, pair) for pair in range(pairs)]

    def products(pair, rows, top):
        s = lax.dot_general(kv_ref[rows, :HD], queries[pair], CONTRACT_LAST, preferred_element_type=f32)
        c = cap_ref[rows, :]
        s = jnp.minimum(s, jnp.concatenate([c, c], axis=1))
        s_buf[pair % 2, rows, :] = s
        dp_buf[pair % 2, rows, :] = lax.dot_general(
            kv_ref[rows, HD:], douts[pair], CONTRACT_LAST, preferred_element_type=f32
        )
        s = fold(s, jnp.max)
        return s if top is None else jnp.maximum(top, s)

    def grads_of(pair, rows):
        if pair == pairs - 1:
            return last_ref.at[rows, :]
        return grads_ref.at[rows, 2 * pair * block : 2 * (pair + 1) * block]

    def sums(pair, rows):
        probs = p_buf[pair % 2, rows, :]
        grads = grads_of(pair, rows)[...]
        dv = jnp.dot(probs, douts[pair], preferred_element_type=f32)
        dk = jnp.dot(grads, queries[pair], preferred_element_type=f32)
        if pair > 0:
            dv, dk = dv + dv_ref[rows, :], dk + dk_ref[rows, :]
        if pair < pairs - 1:
            dv_ref[rows, :], dk_ref[rows, :] = dv, dk
        else:
            dkv_ref[rows, :HD] = (dk * root).astype(bf16)
            dkv_ref[rows, HD:] = dv.astype(bf16)

    top = None
    for rows in chunks:
        top = products(0, rows, top)
    for pair in range(pairs):
        top_now = jnp.max(top, axis=0, keepdims=True)
        total = jnp.zeros((8, 2 * block), f32)
        dot = jnp.zeros((8, 2 * block), f32)
        top = None
        for rows in chunks:
            if pair + 1 < pairs:
                top = products(pair + 1, rows, top)
            e = jnp.exp2((s_buf[pair % 2, rows, :] - top_now) * to_exp2)
            s_buf[pair % 2, rows, :] = e
            total += fold(e, jnp.sum)
            dot += fold(e * dp_buf[pair % 2, rows, :], jnp.sum)
        inverse = 1.0 / jnp.sum(total, axis=0, keepdims=True)
        row_dot = jnp.sum(dot, axis=0, keepdims=True) * inverse
        for rows in chunks:
            if pair > 0:
                sums(pair - 1, rows)
            p = s_buf[pair % 2, rows, :] * inverse
            p_buf[pair % 2, rows, :] = p.astype(bf16)
            grads = p * (dp_buf[pair % 2, rows, :] - row_dot)
            grads_of(pair, rows)[...] = grads.astype(bf16)
    for rows in chunks:
        sums(pairs - 1, rows)
    dquery_of(kv_ref[:, :HD].T, last_ref[...], dq_last_ref)


def dquery_of(keys_t, grads, dq_ref):
    block = dq_ref.shape[0]
    dq_t = jnp.dot(keys_t, grads, preferred_element_type=jnp.float32) * (1.0 / math.sqrt(HD))
    for h in range(grads.shape[1] // block):
        cols = slice(h * HD, (h + 1) * HD)
        dq_ref[:, cols] = dq_t[:, h * block : (h + 1) * block].T.astype(jnp.bfloat16)


def dquery_kernel(kv_ref, grads_ref, dq_last_ref, dq_ref):
    split = dq_ref.shape[1] - dq_last_ref.shape[1]
    dquery_of(kv_ref[:, :HD].T, grads_ref[...], dq_ref.at[:, :split])
    dq_ref[:, split:] = dq_last_ref[...]


def part_sum(parts_ref, g, keep):
    groups = parts_ref.shape[0] // ROW
    total = None
    for j in range(ROW):
        part = parts_ref[j * groups + g].astype(jnp.float32)
        part = jnp.where(keep(j), part, 0.0)
        total = part if total is None else total + part
    return total


def prev_sum_kernel(parts_ref, prev_ref):
    groups = prev_ref.shape[0]
    count = jnp.where(lax.axis_index("z") > 0, lax.axis_index("j"), 0)

    def add(j, sums):
        return tuple(
            total + parts_ref[j * groups + g].astype(jnp.float32) for g, total in enumerate(sums)
        )

    zero = jnp.zeros(prev_ref.shape[1:], jnp.float32)
    for g, total in enumerate(lax.fori_loop(0, count, add, (zero,) * groups)):
        prev_ref[g] = total.astype(jnp.bfloat16)


def own_sum_kernel(parts_ref, own_ref):
    jp = lax.axis_index("j")
    for g in range(own_ref.shape[0]):
        own_ref[g] = part_sum(parts_ref, g, lambda j: j >= jp)


def join_kernel(own_ref, next_ref, dkey_ref, dvalue_ref):
    for g in range(own_ref.shape[0]):
        cols = slice(g * HD, (g + 1) * HD)
        both = own_ref[g] + next_ref[g].astype(jnp.float32)
        dkey_ref[:, cols] = both[:, :HD].astype(jnp.bfloat16)
        dvalue_ref[:, cols] = both[:, HD:].astype(jnp.bfloat16)


def held(array):
    return pltpu.with_memory_space_constraint(array, pltpu.VMEM)


def off_chip(array):
    return pltpu.with_memory_space_constraint(array, pltpu.HBM)


def shards(query, key, value, dout, doc_ids, pair_flags):
    bf16, f32 = jnp.bfloat16, jnp.float32
    tokens, width = key.shape
    groups = width // HD
    block = query.shape[0]
    slots = ROW * groups
    rows = lax.axis_size("z")
    mine, doc_rows, flags, query, dout = pl.pallas_call(
        pack_kernel,
        out_shape=(
            pltpu.VMEM((tokens, 2 * width), bf16),
            pltpu.VMEM((2, ROW, block), jnp.int32),
            pltpu.VMEM(pair_flags.shape, jnp.int32),
            pltpu.VMEM(query.shape, bf16),
            pltpu.VMEM(dout.shape, bf16),
        ),
        in_specs=[HBM] * 6,
        out_specs=(VMEM,) * 5,
        scratch_shapes=[pltpu.SemaphoreType.DMA((7,))],
        compiler_params=pltpu.CompilerParams(vmem_limit_bytes=4 << 20),
        name="pack",
    )(*map(off_chip, (key, value, doc_ids.reshape(-1, block), pair_flags, query, dout)))
    passed = [(z * ROW + j, (z + 1) * ROW + j) for z in range(rows - 1) for j in range(1, ROW)]
    prev = lax.ppermute(mine, ("z", "j"), passed)
    first_row = (lax.axis_index("z") == 0).astype(jnp.int32)
    prev, first_row = lax.optimization_barrier((prev, first_row))
    sent = pl.pallas_call(
        spread_kernel,
        out_shape=pltpu.VMEM((slots, tokens, 2 * HD), bf16),
        in_specs=[VMEM, VMEM],
        out_specs=VMEM,
        compiler_params=pltpu.CompilerParams(vmem_limit_bytes=4 << 20),
        name="spread",
    )(held(mine), held(prev))
    taken = lax.all_to_all(sent, ("j", "head"), 0, 0, tiled=True)
    taken, first_row = lax.optimization_barrier((taken, first_row))
    taken = taken.reshape(ROW * block, 2 * HD)
    parts, grads, dq_last = pl.pallas_call(
        attention_kernel,
        out_shape=(
            pltpu.VMEM((ROW * block, 2 * HD), bf16),
            pltpu.VMEM((ROW * block, (QPK - 2) * block), bf16),
            pltpu.VMEM((block, 2 * HD), bf16),
        ),
        in_specs=[VMEM, VMEM, VMEM, VMEM, VMEM],
        out_specs=(VMEM, VMEM, VMEM),
        scratch_shapes=[
            pltpu.VMEM((ROW * block, block), f32),
            pltpu.VMEM((2, ROW * block, 2 * block), f32),
            pltpu.VMEM((2, ROW * block, 2 * block), f32),
            pltpu.VMEM((2, ROW * block, 2 * block), bf16),
            pltpu.VMEM((ROW * block, HD), f32),
            pltpu.VMEM((ROW * block, HD), f32),
            pltpu.VMEM((ROW * block, 2 * block), bf16),
        ],
        compiler_params=pltpu.CompilerParams(vmem_limit_bytes=32 << 20),
        name="attention",
    )(held(doc_rows), held(flags), held(query), held(dout), held(taken))
    exchange = lambda a: lax.all_to_all(a, ("j", "head"), 0, 0, tiled=True)
    parts = parts.reshape(slots, tokens, 2 * HD)
    back = lax.switch(first_row, (exchange, lambda a: a), parts)
    dquery = pl.pallas_call(
        dquery_kernel,
        out_shape=jax.ShapeDtypeStruct(query.shape, bf16),
        in_specs=[VMEM, VMEM, VMEM],
        out_specs=VMEM,
        compiler_params=pltpu.CompilerParams(vmem_limit_bytes=8 << 20),
        name="dquery",
    )(held(taken), held(grads), held(dq_last))
    to_prev = pl.pallas_call(
        prev_sum_kernel,
        out_shape=pltpu.VMEM((groups, tokens, 2 * HD), bf16),
        in_specs=[VMEM],
        out_specs=VMEM,
        compiler_params=pltpu.CompilerParams(vmem_limit_bytes=4 << 20),
        name="prev_sum",
    )(held(back))
    to_prev, back = lax.optimization_barrier((to_prev, back))
    from_next = lax.ppermute(to_prev, ("z", "j"), [(b, a) for a, b in passed])
    back = lax.switch(first_row, (lambda b: b, exchange), back)
    own = pl.pallas_call(
        own_sum_kernel,
        out_shape=pltpu.VMEM((groups, tokens, 2 * HD), f32),
        in_specs=[VMEM],
        out_specs=VMEM,
        compiler_params=pltpu.CompilerParams(vmem_limit_bytes=4 << 20),
        name="own_sum",
    )(held(back))
    dkey, dvalue = pl.pallas_call(
        join_kernel,
        out_shape=(
            jax.ShapeDtypeStruct(key.shape, bf16),
            jax.ShapeDtypeStruct(value.shape, bf16),
        ),
        in_specs=[VMEM, VMEM],
        out_specs=(VMEM, VMEM),
        compiler_params=pltpu.CompilerParams(vmem_limit_bytes=4 << 20),
        name="join",
    )(held(own), held(from_next))
    return (dquery, dkey, dvalue)


def solution(mesh):
    ctx, head = mesh.shape["ctx"], mesh.shape["head"]
    fine = Mesh(mesh.devices.reshape(ctx // ROW, ROW, head), ("z", "j", "head"))
    by_token = P(("z", "j", "head"), None)
    in_specs = (
        P(("z", "j"), "head"),
        by_token,
        by_token,
        P(("z", "j"), "head"),
        P(),
        P(("z", "j"), None),
    )
    out_specs = (P(("z", "j"), "head"), by_token, by_token)
    return jax.shard_map(shards, mesh=fine, in_specs=in_specs, out_specs=out_specs, check_vma=False)
```
